512 devices in a mesh: dp: 64 (over z, x_lo, core), lon: 8 (over y, x_hi).
Axes of the slice: x: 4 (x_hi: 2, x_lo: 2; x = x_hi * 2 + x_lo), y: 4, z: 16, core: 2. Of those that a mesh axis runs over, the one named last changes fastest.
Arguments:
- features: bfloat16 [64, 72, 48, 1152], P('dp', 'lon'), may hold values from -6 to 6
- depth_w: bfloat16 [2, 3, 3, 1152], replicated, may hold values from -2 to 2
- point_w: bfloat16 [2, 1152, 256], replicated, may hold values from -0.1875 to 0.1875
- point_bias: float32 [2, 256], replicated, may hold values from -3 to 3
- cotangent: bfloat16 [64, 72, 48, 512], P('dp', 'lon'), may hold values from -6 to 6
Outputs:
- feature_grad: bfloat16 [64, 72, 48, 1152], P('dp', 'lon')
- depth_grad: bfloat16 [2, 3, 3, 1152], replicated
- point_grad: bfloat16 [2, 1152, 256], replicated
- bias_grad: float32 [2, 256], replicated
The draws below stay inside these ranges and needn't reach their ends.
All inputs are finite; a program needn't handle non-finite values.
Results may differ from the reference program's by a relative error of at most 0.0075.
Values may be sent and summed in bfloat16 or wider, within the bound.
No kernel may reach another device: no remote copies, remote signals or barrier semaphores. Data moves between devices by JAX's collectives and lax.ppermute only.
A program may use at most 128 MiB of HBM per device.

```python
import jax
import jax.numpy as jnp
from jax import lax

LAT = 48
C = 1152
C_OUT = 256
RATE_A = 24
RATE_B = 36
IMGS = 64
LON = 72


def block_levels(stream_key, extent, pieces, low, top_value):
    loudness = 1.0
    for axis_at, parts in pieces:
        heights = jax.random.uniform(jax.random.fold_in(jax.random.fold_in(stream_key, 6), axis_at), (parts,), jnp.float32, low / len(pieces), top_value / len(pieces))
        loudness = loudness * jnp.repeat(jnp.exp(heights), extent[axis_at] // parts).reshape((-1,) + (1,) * (len(extent) - 1 - axis_at))
    return loudness


def gaussian(own_key, shape, scale, most, split=(), kind=jnp.bfloat16):
    gain = block_levels(own_key, shape, split, -0.22, 0.18) if split else 1.0
    drawn = jax.random.normal(own_key, shape, jnp.float32) * scale * gain
    return jnp.minimum(jnp.maximum(drawn, -most), most).astype(kind)


def setup_inputs(seed: int = 0) -> dict:
    arg_keys = jax.random.split(jax.random.key(seed), 6)
    features = gaussian(arg_keys[0], (IMGS, LON, LAT, C), 1.0, 6.0, ((0, 64), (1, 8)))
    depth_w = gaussian(arg_keys[1], (2, 3, 3, C), 9 ** -0.5, 2.0)
    point_w = gaussian(arg_keys[2], (2, C, C_OUT), C ** -0.5, 0.1875)
    point_bias = gaussian(arg_keys[3], (2, C_OUT), 0.5, 3.0, (), jnp.float32)
    cotangent = gaussian(arg_keys[4], (IMGS, LON, LAT, 2 * C_OUT), 1.0, 6.0, ((0, 64), (1, 8)))
    return {"features": features, "depth_w": depth_w, "point_w": point_w, "point_bias": point_bias, "cotangent": cotangent}


def lat_shift(grid_field, offset, axis_pos):
    height = grid_field.shape[axis_pos]
    if offset == 0:
        return grid_field
    if abs(offset) >= height:
        return jnp.zeros_like(grid_field)
    widths = [(0, 0)] * grid_field.ndim
    if offset > 0:
        kept_rows = lax.slice_in_dim(grid_field, offset, height, axis=axis_pos)
        widths[axis_pos] = (0, offset)
    else:
        kept_rows = lax.slice_in_dim(grid_field, 0, height + offset, axis=axis_pos)
        widths[axis_pos] = (-offset, 0)
    return jnp.pad(kept_rows, widths)


def gate_slope(pre_act):
    sigmoid_val = jax.nn.sigmoid(pre_act)
    return sigmoid_val * (1.0 + pre_act * (1.0 - sigmoid_val))


def reference(features, depth_w, point_w, point_bias, cotangent):
    dilations = (RATE_A, RATE_B)

    def one_image(totals, inputs):
        point_total, depth_total, bias_total = totals
        image_cells, upstream = inputs
        channels = image_cells.shape[2]
        outputs = point_w.shape[2]
        grad_field = jnp.zeros(image_cells.shape, jnp.float32)
        point_new = []
        depth_new = []
        bias_new = []
        for branch, dilation in enumerate(dilations):
            moved_taps = {}
            depth_acc = jnp.zeros(image_cells.shape, jnp.float32)
            for lon_step in (-1, 0, 1):
                rolled = jnp.roll(image_cells, -lon_step * dilation, axis=0)
                for lat_step in (-1, 0, 1):
                    tapped = lat_shift(rolled, lat_step * dilation, 1).astype(jnp.float32)
                    moved_taps[(lat_step, lon_step)] = tapped
                    depth_acc = depth_acc + depth_w[branch, lat_step + 1, lon_step + 1].astype(jnp.float32) * tapped
            depth_out = depth_acc.astype(jnp.bfloat16)
            flat_depth = depth_out.reshape(-1, channels)
            point_act = jnp.dot(flat_depth, point_w[branch], preferred_element_type=jnp.float32) + point_bias[branch]
            upstream_part = upstream[:, :, branch * outputs:(branch + 1) * outputs].reshape(-1, outputs).astype(jnp.float32)
            pgrad = (upstream_part * gate_slope(point_act)).astype(jnp.bfloat16)
            bias_new.append(bias_total[branch] + jnp.sum(pgrad.astype(jnp.float32), axis=0))
            point_new.append(point_total[branch] + jnp.dot(flat_depth.T, pgrad, preferred_element_type=jnp.float32))
            dgrad = jnp.dot(pgrad, point_w[branch].T, preferred_element_type=jnp.float32).astype(jnp.bfloat16)
            dgrad = dgrad.reshape(image_cells.shape)
            dgrad_wide = dgrad.astype(jnp.float32)
            tap_rows = []
            for lat_step in (-1, 0, 1):
                tap_cols = []
                for lon_step in (-1, 0, 1):
                    tap_cols.append(jnp.sum(moved_taps[(lat_step, lon_step)] * dgrad_wide, axis=(0, 1)))
                    behind = lat_shift(jnp.roll(dgrad, lon_step * dilation, axis=0), -lat_step * dilation, 1)
                    grad_field = grad_field + depth_w[branch, lat_step + 1, lon_step + 1].astype(jnp.float32) * behind.astype(jnp.float32)
                tap_rows.append(jnp.stack(tap_cols))
            depth_new.append(depth_total[branch] + jnp.stack(tap_rows))
        new_totals = (jnp.stack(point_new), jnp.stack(depth_new), jnp.stack(bias_new))
        return new_totals, grad_field.astype(jnp.bfloat16)

    start_totals = (jnp.zeros((2, C, C_OUT), jnp.float32), jnp.zeros((2, 3, 3, C), jnp.float32), jnp.zeros((2, C_OUT), jnp.float32))
    final_totals, feature_grad = lax.scan(one_image, start_totals, (features, cotangent))
    point_total, depth_total, bias_total = final_totals
    depth_grad = (depth_total / IMGS).astype(jnp.bfloat16)
    point_grad = (point_total / IMGS).astype(jnp.bfloat16)
    bias_grad = bias_total / IMGS
    return (feature_grad, depth_grad, point_grad, bias_grad)
```

```python
import jax
import jax.numpy as jnp
from jax import lax
from jax.sharding import Mesh
from jax.sharding import PartitionSpec as P

RATE_A = 24
RATE_B = 36


def from_behind(block, axis, distance):
    devices = range(lax.axis_size(axis))
    route = [((i - distance) % len(devices), i) for i in devices]
    return lax.ppermute(block, axis, route)


def lat_shift(grid_field, offset, axis_pos):
    height = grid_field.shape[axis_pos]
    if offset == 0:
        return grid_field
    widths = [(0, 0)] * grid_field.ndim
    if offset > 0:
        kept_rows = lax.slice_in_dim(grid_field, offset, height, axis=axis_pos)
        widths[axis_pos] = (0, offset)
    else:
        kept_rows = lax.slice_in_dim(grid_field, 0, height + offset, axis=axis_pos)
        widths[axis_pos] = (-offset, 0)
    return jnp.pad(kept_rows, widths)


def gate_slope(pre_act):
    sigmoid_val = jax.nn.sigmoid(pre_act)
    return sigmoid_val * (1.0 + pre_act * (1.0 - sigmoid_val))


def column_plan(dilation, direction, columns, group_size):
    run_list = []
    for column in range(columns):
        target = column + direction * dilation
        offset = target // columns
        local_col = target % columns
        if run_list and run_list[-1][0] == offset:
            run_list[-1][2] = local_col + 1
        else:
            run_list.append([offset, local_col, local_col + 1])
    return [(-entry[0] % group_size, entry[1], entry[2]) for entry in run_list]


def join_pieces(piece_list):
    if len(piece_list) == 1:
        return piece_list[0]
    return jnp.concatenate(piece_list, axis=1)


def fetch_each(grid_field, offset_pairs, group_size, send_fn):
    result = {}
    for offset_pair in offset_pairs:
        piece_list = []
        for shift_by, first_col, finish in column_plan(
            offset_pair[0], offset_pair[1], grid_field.shape[1], group_size
        ):
            column_piece = grid_field[:, first_col:finish]
            column_piece = send_fn(column_piece, shift_by)
            piece_list.append(column_piece)
        result[offset_pair] = join_pieces(piece_list)
    return result


def send_features(column_piece, shift_by):
    return from_behind(column_piece, LON, shift_by)


def send_grads(column_piece, shift_by):
    return from_behind(column_piece, LON, shift_by)


DP = ("z", "xl", "core")
LON = ("y", "xh")
PLANE = ("xl", "y", "xh")
LANES = 128


def swap_cores(block):
    return lax.ppermute(block, "core", [(0, 1), (1, 0)])


def exchange(blocks, axes):
    return lax.all_to_all(blocks, axes, 0, 0, tiled=True)


def gather_copies(block, axes):
    peers = lax.axis_size(axes)
    return exchange(jnp.broadcast_to(block[None], (peers,) + block.shape), axes)


def sum_over_mesh(point_local, depth_local, bias_local, images):
    branches, channels, outputs = point_local.shape
    plane = lax.axis_size(PLANE)
    depth = lax.axis_size("z")
    main = point_local.reshape(branches, channels, 2, outputs // 2)
    main = main.transpose(2, 0, 1, 3).reshape(2, plane, -1, LANES)
    small = jnp.concatenate([depth_local.reshape(-1), bias_local.reshape(-1)])
    unit = 2 * plane * LANES
    main_rows = main.shape[2]
    small_rows = -(-small.size // unit)
    rows = -(-(main_rows + small_rows) // depth) * depth
    small_rows = rows - main_rows
    small = jnp.pad(small, (0, small_rows * unit - small.size)).reshape(2, plane, -1, LANES)
    terms = jnp.concatenate([main, small], axis=2)
    core = lax.axis_index("core")
    kept = lax.dynamic_index_in_dim(terms, core, 0, keepdims=False)
    sent = lax.dynamic_index_in_dim(terms, 1 - core, 0, keepdims=False)
    terms = kept + swap_cores(sent.astype(jnp.bfloat16)).astype(jnp.float32)
    terms = exchange(terms.astype(jnp.bfloat16), PLANE)
    terms = jnp.sum(terms.astype(jnp.float32), axis=0)
    terms = exchange(terms.reshape(depth, rows // depth, LANES), "z")
    total = (jnp.sum(terms, axis=0) / images).astype(jnp.bfloat16)
    total = gather_copies(total, "z").reshape(rows, LANES)
    total = gather_copies(total, PLANE)
    other = swap_cores(total)
    total = jnp.where(core == 0, jnp.stack([total, other]), jnp.stack([other, total]))
    point = total[:, :, :main_rows].reshape(2, branches, channels, outputs // 2)
    point = point.transpose(1, 2, 0, 3).reshape(point_local.shape)
    small = total[:, :, main_rows:].reshape(-1)
    depth_grad = small[: depth_local.size].reshape(depth_local.shape)
    bias = small[depth_local.size : depth_local.size + bias_local.size].reshape(bias_local.shape)
    return point, depth_grad, bias.astype(jnp.float32)


def per_device(features, depth_w, point_w, point_bias, cotangent):
    group_size = lax.axis_size(LON)
    channels = features.shape[3]
    outputs = point_w.shape[2]
    dilations = (RATE_A, RATE_B)
    offset_pairs = [(dilation, direction) for dilation in dilations for direction in (-1, 1)]
    moved_in = fetch_each(features, offset_pairs, group_size, send_features)
    depth_outs = []
    for branch, dilation in enumerate(dilations):
        depth_acc = jnp.zeros(features.shape, jnp.float32)
        for lon_step in (-1, 0, 1):
            source = features if lon_step == 0 else moved_in[dilation, lon_step]
            for lat_step in (-1, 0, 1):
                tapped = lat_shift(source, lat_step * dilation, 2).astype(jnp.float32)
                depth_acc = (
                    depth_acc
                    + depth_w[branch, lat_step + 1, lon_step + 1].astype(jnp.float32) * tapped
                )
        depth_outs.append(depth_acc.astype(jnp.bfloat16))
    point_terms = []
    bias_terms = []
    dgrad_list = []
    for branch, dilation in enumerate(dilations):
        flat_depth = depth_outs[branch].reshape(-1, channels)
        point_act = (
            jnp.dot(flat_depth, point_w[branch], preferred_element_type=jnp.float32)
            + point_bias[branch]
        )
        upstream_part = (
            cotangent[..., branch * outputs : (branch + 1) * outputs]
            .reshape(-1, outputs)
            .astype(jnp.float32)
        )
        pgrad = (upstream_part * gate_slope(point_act)).astype(jnp.bfloat16)
        bias_terms.append(jnp.sum(pgrad.astype(jnp.float32), axis=0))
        point_terms.append(
            lax.dot_general(
                flat_depth, pgrad, (((0,), (0,)), ((), ())), preferred_element_type=jnp.float32
            )
        )
        dgrad = lax.dot_general(
            pgrad, point_w[branch], (((1,), (1,)), ((), ())), preferred_element_type=jnp.float32
        )
        dgrad_list.append(dgrad.astype(jnp.bfloat16).reshape(features.shape))
    point_local = jnp.stack(point_terms)
    bias_local = jnp.stack(bias_terms)
    grad_field = jnp.zeros(features.shape, jnp.float32)
    depth_terms = []
    for branch, dilation in enumerate(dilations):
        branch_pairs = [(dilation, -1), (dilation, 1)]
        moved_back = fetch_each(dgrad_list[branch], branch_pairs, group_size, send_grads)
        dgrad_wide = dgrad_list[branch].astype(jnp.float32)
        tap_rows = []
        for lat_step in (-1, 0, 1):
            tap_cols = []
            for lon_step in (-1, 0, 1):
                source = features if lon_step == 0 else moved_in[dilation, lon_step]
                tapped = lat_shift(source, lat_step * dilation, 2).astype(jnp.float32)
                tap_cols.append(jnp.sum(tapped * dgrad_wide, axis=(0, 1, 2)))
                behind = dgrad_list[branch] if lon_step == 0 else moved_back[dilation, -lon_step]
                behind = lat_shift(behind, -lat_step * dilation, 2).astype(jnp.float32)
                grad_field = (
                    grad_field
                    + depth_w[branch, lat_step + 1, lon_step + 1].astype(jnp.float32) * behind
                )
            tap_rows.append(jnp.stack(tap_cols))
        depth_terms.append(jnp.stack(tap_rows))
    depth_local = jnp.stack(depth_terms)
    feature_grad = grad_field.astype(jnp.bfloat16)
    images = lax.axis_size(DP) * features.shape[0]
    point_grad, depth_grad, bias_grad = sum_over_mesh(point_local, depth_local, bias_local, images)
    return (feature_grad, depth_grad, point_grad, bias_grad)


def solution(mesh):
    fine = Mesh(mesh.devices.reshape(16, 2, 2, 4, 2), DP + LON)
    placed = (P(DP, LON, None, None), P(), P(), P(), P(DP, LON, None, None))
    return jax.shard_map(
        per_device,
        mesh=fine,
        in_specs=placed,
        out_specs=(P(DP, LON, None, None), P(), P(), P()),
        check_vma=False,
    )
```

```python
import jax
import jax.numpy as jnp
from jax import lax
from jax.sharding import Mesh
from jax.sharding import PartitionSpec as P

RATE_A = 24
RATE_B = 36
CLASS = 12
PAIR = 2

DP = ("zh", "zl", "xl", "core")
LON = ("y", "xh")
PLANE = ("xl", "y", "xh")


def swap_cores(block):
    return lax.ppermute(block, "core", [(0, 1), (1, 0)])


def exchange(blocks, axes):
    return lax.all_to_all(blocks, axes, 0, 0, tiled=True)


def gather_copies(block, axes):
    peers = lax.axis_size(axes)
    return exchange(jnp.broadcast_to(block[None], (peers,) + block.shape), axes)


def scatter_sum(terms):
    core = lax.axis_index("core")
    kept = lax.dynamic_index_in_dim(terms, core, 0, keepdims=False)
    sent = lax.dynamic_index_in_dim(terms, 1 - core, 0, keepdims=False)
    terms = kept + swap_cores(sent.astype(jnp.bfloat16)).astype(jnp.float32)
    terms = exchange(terms.astype(jnp.bfloat16), PLANE)
    return jnp.sum(terms.astype(jnp.float32), axis=0)


def sum_over_mesh(point_local, depth_local, bias_local, images):
    branches, channels, outputs = point_local.shape
    plane = lax.axis_size(PLANE)
    main = scatter_sum(point_local.reshape(branches, plane, -1, outputs))
    small = jnp.concatenate([depth_local.reshape(branches, -1), bias_local], axis=1)
    used = small.shape[1]
    unit = plane * 8 * outputs
    room = -(-used // unit) * unit
    small = jnp.pad(small, ((0, 0), (0, room - used))).reshape(branches, plane, -1, outputs)
    small = scatter_sum(small)
    main_rows = main.shape[0]
    terms = jnp.concatenate([main, small], axis=0)
    terms = jnp.sum(gather_copies(terms, "zl"), axis=0)
    terms = jnp.sum(gather_copies(terms.astype(jnp.bfloat16), "zh").astype(jnp.float32), axis=0)
    total = gather_copies((terms / images).astype(jnp.bfloat16), PLANE)
    other = swap_cores(total)
    first = lax.axis_index("core") == 0
    total = jnp.stack([jnp.where(first, total, other), jnp.where(first, other, total)])
    point = total[:, :, :main_rows].reshape(point_local.shape)
    small = total[:, :, main_rows:].reshape(branches, -1)
    depth_grad = small[:, : used - outputs].reshape(depth_local.shape)
    bias = small[:, used - outputs : used].astype(jnp.float32)
    return point, depth_grad, bias


def to_classes(field):
    _, columns, rows, width = field.shape
    peers = lax.axis_size(LON)
    groups = CLASS // PAIR
    chunks = field.reshape(columns, rows // CLASS, groups, PAIR, width).transpose(2, 0, 1, 3, 4)
    chunks = chunks.reshape(groups, columns, rows // groups, width)
    chunks = jnp.pad(chunks, ((0, peers - groups), (0, 0), (0, 0), (0, 0)))
    return exchange(chunks, LON).reshape(peers * columns, rows // groups, width)


def from_classes(field, rows):
    columns, held, width = field.shape
    peers = lax.axis_size(LON)
    groups = CLASS // PAIR
    chunks = exchange(field.reshape(peers, columns // peers, held, width), LON)[:groups]
    chunks = chunks.reshape(groups, columns // peers, rows // CLASS, PAIR, width)
    return chunks.transpose(1, 2, 0, 3, 4).reshape(1, columns // peers, rows, width)


def lat_shift(field, dilation, step):
    if step == 0:
        return field
    height = field.shape[1]
    offset = dilation * PAIR // CLASS
    if step > 0:
        return jnp.pad(field[:, offset:], ((0, 0), (0, offset), (0, 0)))
    return jnp.pad(field[:, : height - offset], ((0, 0), (offset, 0), (0, 0)))


def gate_slope(pre_act):
    sigmoid_val = jax.nn.sigmoid(pre_act)
    return sigmoid_val * (1.0 + pre_act * (1.0 - sigmoid_val))


def per_device(features, depth_w, point_w, point_bias, cotangent):
    rows = features.shape[2]
    outputs = point_w.shape[2]
    dilations = (RATE_A, RATE_B)
    images = lax.axis_size(DP) * features.shape[0]
    taps = depth_w.astype(jnp.float32)
    field = to_classes(features)
    upstream = to_classes(cotangent)
    columns, held, channels = field.shape
    point_terms = []
    bias_terms = []
    dgrad_list = []
    for branch, dilation in enumerate(dilations):
        depth_acc = jnp.zeros(field.shape, jnp.float32)
        for lon_step in (-1, 0, 1):
            source = jnp.roll(field, -lon_step * dilation, axis=0)
            for lat_step in (-1, 0, 1):
                tapped = lat_shift(source, dilation, lat_step).astype(jnp.float32)
                depth_acc = depth_acc + taps[branch, lat_step + 1, lon_step + 1] * tapped
        flat_depth = depth_acc.astype(jnp.bfloat16).reshape(-1, channels)
        point_act = (
            jnp.dot(flat_depth, point_w[branch], preferred_element_type=jnp.float32)
            + point_bias[branch]
        )
        upstream_part = (
            upstream[..., branch * outputs : (branch + 1) * outputs]
            .reshape(-1, outputs)
            .astype(jnp.float32)
        )
        pgrad = (upstream_part * gate_slope(point_act)).astype(jnp.bfloat16)
        bias_terms.append(jnp.sum(pgrad.astype(jnp.float32), axis=0))
        point_terms.append(
            lax.dot_general(
                flat_depth, pgrad, (((0,), (0,)), ((), ())), preferred_element_type=jnp.float32
            )
        )
        dgrad = lax.dot_general(
            pgrad, point_w[branch], (((1,), (1,)), ((), ())), preferred_element_type=jnp.float32
        )
        dgrad_list.append(dgrad.astype(jnp.bfloat16).reshape(field.shape))
    grad_field = jnp.zeros(field.shape, jnp.float32)
    depth_terms = []
    for branch, dilation in enumerate(dilations):
        dgrad_wide = dgrad_list[branch].astype(jnp.float32)
        tap_rows = []
        for lat_step in (-1, 0, 1):
            tap_cols = []
            for lon_step in (-1, 0, 1):
                source = jnp.roll(field, -lon_step * dilation, axis=0)
                tapped = lat_shift(source, dilation, lat_step).astype(jnp.float32)
                tap_cols.append(jnp.sum(tapped * dgrad_wide, axis=(0, 1)))
                behind = jnp.roll(dgrad_list[branch], lon_step * dilation, axis=0)
                behind = lat_shift(behind, dilation, -lat_step).astype(jnp.float32)
                grad_field = grad_field + taps[branch, lat_step + 1, lon_step + 1] * behind
            tap_rows.append(jnp.stack(tap_cols))
        depth_terms.append(jnp.stack(tap_rows))
    feature_grad = from_classes(grad_field.astype(jnp.bfloat16), rows)
    point_grad, depth_grad, bias_grad = sum_over_mesh(
        jnp.stack(point_terms), jnp.stack(depth_terms), jnp.stack(bias_terms), images
    )
    return (feature_grad, depth_grad, point_grad, bias_grad)


def solution(mesh):
    fine = Mesh(mesh.devices.reshape(4, 4, 2, 2, 4, 2), DP + LON)
    placed = (P(DP, LON, None, None), P(), P(), P(), P(DP, LON, None, None))
    return jax.shard_map(
        per_device,
        mesh=fine,
        in_specs=placed,
        out_specs=(P(DP, LON, None, None), P(), P(), P()),
        check_vma=False,
    )
```

```python
import jax
import jax.numpy as jnp
from jax import lax
from jax.experimental import pallas as pl
from jax.experimental.pallas import tpu as pltpu
from jax.sharding import Mesh
from jax.sharding import PartitionSpec as P

CLASS = 12
PAIR = 2
HELD = 8
LANES = 128

DP = ("zh", "zl", "xl", "core")
LON = ("y", "xh")
PLANE = ("xl", "y", "xh")


def swap_cores(block):
    return lax.ppermute(block, "core", [(0, 1), (1, 0)])


def exchange(blocks, axes):
    return lax.all_to_all(blocks, axes, 0, 0, tiled=True)


def gather_copies(block, axes):
    peers = lax.axis_size(axes)
    return exchange(jnp.broadcast_to(block[None], (peers,) + block.shape), axes)


def sum_four(own, axis):
    near, far, last = [
        lax.ppermute(own, axis, [(i, i ^ m) for i in range(4)]).astype(jnp.float32) for m in (1, 2, 3)
    ]
    return (own.astype(jnp.float32) + near) + (far + last)


def gate_slope(pre_act):
    sigmoid_val = jax.nn.sigmoid(pre_act)
    return sigmoid_val * (1.0 + pre_act * (1.0 - sigmoid_val))


def half_turn(tile):
    return pltpu.roll(tile, 4, 0)


def ends_swapped(tile, top):
    return jnp.where(top, pltpu.roll(tile, 2, 0), pltpu.roll(tile, 6, 0))


def shard_row(row, main, extra):
    return (row // extra) * (main + extra) + main + row % extra


def local_body(core_ref, cls_ref, taps_ref, pw_ref, pb_ref, kept_ref, sent_ref, fg_ref, depth, dgr, terms):
    channels, outputs = pw_ref.shape[1:]
    shard = terms.shape[1] // 16
    main = channels // 16
    extra = shard - main
    tiles = channels // LANES
    wide = outputs // LANES
    per_tap = -(-tiles // wide)
    sub = lax.broadcasted_iota(jnp.int32, (HELD, LANES), 0)
    top = sub < 4
    first = sub < 2
    end = sub >= 6

    def tap(branch, a, e, lanes):
        row = branch * 9 + (a + 1) * 3 + e + 1
        return jnp.broadcast_to(taps_ref[row : row + 1, lanes], (HELD, LANES))

    def ends(up, down):
        return jnp.where(first, up, jnp.where(end, down, 0.0))

    def both(branch, a, lanes):
        return tap(branch, a, -1, lanes) + tap(branch, a, 1, lanes)

    def read(ref, step, lanes, branch=None):
        out = []
        for k in range(6):
            rows = pl.ds(pl.multiple_of(k * 96 + step * 16, 16), 16)
            tile = (ref[rows, lanes] if branch is None else ref[branch, rows, lanes]).astype(jnp.float32)
            out.append((tile[:HELD], tile[HELD:]))
        return [[pair[h] for pair in out] for h in range(2)]

    for t in range(tiles):
        lanes = slice(t * LANES, (t + 1) * LANES)
        mid_a = [tap(0, 0, e, lanes) for e in (-1, 0, 1)]
        off_a = [jnp.where(top, tap(0, 1, e, lanes), tap(0, -1, e, lanes)) for e in (-1, 0, 1)]
        mid_b = [tap(1, 0, 0, lanes), both(1, 0, lanes)]
        off_b = [
            ends(tap(1, 1, 0, lanes), tap(1, -1, 0, lanes)),
            ends(both(1, 1, lanes), both(1, -1, lanes)),
        ]

        def forward(step, carry):
            made_a, made_b = [], []
            for xs in read(cls_ref, step, lanes):
                turned = [half_turn(x) for x in xs]
                swapped = [ends_swapped(x, top) for x in xs]
                made_a.append(
                    [
                        sum(
                            mid_a[n] * xs[(k + 2 * n - 2) % 6] + off_a[n] * turned[(k + 2 * n - 2) % 6]
                            for n in range(3)
                        )
                        for k in range(6)
                    ]
                )
                made_b.append(
                    [
                        mid_b[0] * xs[k]
                        + mid_b[1] * xs[(k + 3) % 6]
                        + off_b[0] * swapped[k]
                        + off_b[1] * swapped[(k + 3) % 6]
                        for k in range(6)
                    ]
                )
            for k in range(6):
                rows = pl.ds(pl.multiple_of(k * 96 + step * 16, 16), 16)
                for branch, made in enumerate((made_a, made_b)):
                    tile = jnp.concatenate([made[0][k], made[1][k]], axis=0)
                    depth[branch, rows, lanes] = tile.astype(jnp.bfloat16)
            return carry

        lax.fori_loop(0, 6, forward, 0)

    for branch in range(2):
        act = jnp.dot(depth[branch], pw_ref[branch], preferred_element_type=jnp.float32)
        act = act + pb_ref[branch : branch + 1, :]
        start = channels + branch * outputs
        up = cls_ref[:, start : start + outputs].astype(jnp.float32)
        pgrad = (up * gate_slope(act)).astype(jnp.bfloat16)
        point = lax.dot_general(
            depth[branch], pgrad, (((0,), (0,)), ((), ())), preferred_element_type=jnp.float32
        )
        for p in range(16):
            terms[branch, p * shard : p * shard + main, :] = point[p * main : (p + 1) * main]
            terms[branch, p * shard + main : (p + 1) * shard, :] = jnp.zeros((extra, outputs), jnp.float32)
        row = shard_row(9 * per_tap, main, extra)
        terms[branch, row : row + 1, :] = jnp.sum(pgrad.astype(jnp.float32), axis=0, keepdims=True)
        for c in range(0, channels, 384):
            part = lax.dot_general(
                pgrad, pw_ref[branch, c : c + 384, :], (((1,), (1,)), ((), ())), preferred_element_type=jnp.float32
            )
            dgr[branch, :, c : c + 384] = part.astype(jnp.bfloat16)

    for t in range(tiles):
        lanes = slice(t * LANES, (t + 1) * LANES)
        mid_a = [tap(0, 0, e, lanes) for e in (-1, 0, 1)]
        off_a = [jnp.where(top, tap(0, -1, e, lanes), tap(0, 1, e, lanes)) for e in (-1, 0, 1)]
        mid_b = [tap(1, 0, 0, lanes), both(1, 0, lanes)]
        off_b = [
            ends(tap(1, -1, 0, lanes), tap(1, 1, 0, lanes)),
            ends(both(1, -1, lanes), both(1, 1, lanes)),
        ]

        def backward(step, sums):
            sums = list(sums)
            made = []
            sides = zip(read(cls_ref, step, lanes), read(dgr, step, lanes, 0), read(dgr, step, lanes, 1))
            for xs, das, dbs in sides:
                turned = [half_turn(d) for d in das]
                swapped = [ends_swapped(d, top) for d in dbs]
                made.append(
                    [
                        sum(
                            mid_a[n] * das[(k - 2 * n + 2) % 6] + off_a[n] * turned[(k - 2 * n + 2) % 6]
                            for n in range(3)
                        )
                        + mid_b[0] * dbs[k]
                        + mid_b[1] * dbs[(k + 3) % 6]
                        + off_b[0] * swapped[k]
                        + off_b[1] * swapped[(k + 3) % 6]
                        for k in range(6)
                    ]
                )
                for n in range(3):
                    sums[n] += sum(xs[(k + 2 * n - 2) % 6] * das[k] for k in range(6))
                    sums[3 + n] += sum(xs[(k + 2 * n - 2) % 6] * turned[k] for k in range(6))
                for n in range(2):
                    sums[6 + n] += sum(xs[(k + 3 * n) % 6] * dbs[k] for k in range(6))
                    sums[8 + n] += sum(xs[(k + 3 * n) % 6] * swapped[k] for k in range(6))
            for k in range(6):
                rows = pl.ds(pl.multiple_of(k * 96 + step * 16, 16), 16)
                fg_ref[rows, lanes] = jnp.concatenate([made[0][k], made[1][k]], axis=0).astype(jnp.bfloat16)
            return tuple(sums)

        sums = lax.fori_loop(0, 6, backward, tuple(jnp.zeros((HELD, LANES), jnp.float32) for _ in range(10)))

        def keep(branch, a, e, value, mask=None):
            value = value if mask is None else jnp.where(mask, value, 0.0)
            row = shard_row(((a + 1) * 3 + e + 1) * per_tap + t // wide, main, extra)
            at = (t % wide) * LANES
            terms[branch, row : row + 1, at : at + LANES] = jnp.sum(value, axis=0, keepdims=True)

        for n in range(3):
            keep(0, 0, n - 1, sums[n])
            keep(0, 1, n - 1, sums[3 + n], jnp.logical_not(top))
            keep(0, -1, n - 1, sums[3 + n], top)
        for e in (-1, 0, 1):
            keep(1, 0, e, sums[6 + abs(e)])
            keep(1, 1, e, sums[8 + abs(e)], end)
            keep(1, -1, e, sums[8 + abs(e)], first)

    @pl.when(core_ref[0] == 0)
    def _():
        kept_ref[...] = terms[0]
        sent_ref[...] = terms[1].astype(jnp.bfloat16)

    @pl.when(core_ref[0] != 0)
    def _():
        kept_ref[...] = terms[1]
        sent_ref[...] = terms[0].astype(jnp.bfloat16)


def local_work(core, field, taps, point_w, point_bias):
    cells = field.shape[0]
    branches, channels, outputs = point_w.shape
    rows = 16 * (channels // 16 + 8)
    vmem = pl.BlockSpec(memory_space=pltpu.VMEM)
    return pl.pallas_call(
        local_body,
        out_shape=(
            jax.ShapeDtypeStruct((rows, outputs), jnp.float32),
            jax.ShapeDtypeStruct((rows, outputs), jnp.bfloat16),
            jax.ShapeDtypeStruct((cells, channels), jnp.bfloat16),
        ),
        in_specs=[pl.BlockSpec(memory_space=pltpu.SMEM)] + [vmem] * 4,
        out_specs=(vmem, vmem, vmem),
        scratch_shapes=[
            pltpu.VMEM((branches, cells, channels), jnp.bfloat16),
            pltpu.VMEM((branches, cells, channels), jnp.bfloat16),
            pltpu.VMEM((branches, rows, outputs), jnp.float32),
        ],
        compiler_params=pltpu.CompilerParams(vmem_limit_bytes=48 << 20),
        name="local_work",
    )(core, field, taps, point_w, point_bias)


def to_chunks(field):
    _, columns, rows, width = field.shape
    groups = CLASS // PAIR
    chunks = field.reshape(columns, rows // CLASS, groups, PAIR, width).transpose(2, 0, 1, 3, 4)
    return chunks.reshape(groups, columns, rows // groups, width)


def per_device(features, depth_w, point_w, point_bias, cotangent):
    _, columns, rows, channels = features.shape
    branches, _, outputs = point_w.shape
    images = lax.axis_size(DP) * features.shape[0]
    peers = lax.axis_size(LON)
    plane = lax.axis_size(PLANE)
    groups = CLASS // PAIR
    core = lax.axis_index("core")

    chunks = jnp.concatenate([to_chunks(features), to_chunks(cotangent)], axis=3)
    chunks = jnp.pad(chunks, ((0, peers - groups), (0, 0), (0, 0), (0, 0)))
    field = exchange(chunks, LON).reshape(peers * columns * HELD, chunks.shape[3])
    taps = depth_w.astype(jnp.float32).reshape(branches * 9, channels)
    kept, sent, fgrad = local_work(core.reshape(1), field, taps, point_w, point_bias)

    terms = (kept + swap_cores(sent).astype(jnp.float32)).astype(jnp.bfloat16)
    shard = terms.shape[0] // plane
    terms = exchange(terms.reshape(plane, shard, outputs), PLANE)
    fgrad, terms = lax.optimization_barrier((fgrad, terms))
    fgrad = exchange(fgrad.reshape(peers, columns, HELD, channels), LON)
    terms = jnp.sum(terms.astype(jnp.float32), axis=0)
    terms = sum_four(terms, "zl").astype(jnp.bfloat16)
    total = (sum_four(terms, "zh") / images).astype(jnp.bfloat16)
    fgrad, total = lax.optimization_barrier((fgrad, total))
    total = gather_copies(total, PLANE)
    other = swap_cores(total)
    total = jnp.stack([jnp.where(core == 0, total, other), jnp.where(core == 0, other, total)])

    main = channels // plane
    point_grad = total[:, :, :main].reshape(point_w.shape)
    small = total[:, :, main:].reshape(branches, -1, outputs)
    per_tap = -(-channels // outputs)
    depth_grad = small[:, : 9 * per_tap].reshape(branches, 9, -1)[:, :, :channels].reshape(depth_w.shape)
    bias_grad = small[:, 9 * per_tap].astype(jnp.float32)
    fgrad = fgrad[:groups].reshape(groups, columns, rows // CLASS, PAIR, channels)
    feature_grad = fgrad.transpose(1, 2, 0, 3, 4).reshape(features.shape)
    return (feature_grad, depth_grad, point_grad, bias_grad)


def solution(mesh):
    fine = Mesh(mesh.devices.reshape(4, 4, 2, 2, 4, 2), DP + LON)
    placed = (P(DP, LON, None, None), P(), P(), P(), P(DP, LON, None, None))
    return jax.shard_map(
        per_device,
        mesh=fine,
        in_specs=placed,
        out_specs=(P(DP, LON, None, None), P(), P(), P()),
        check_vma=False,
    )
```

```python
import jax
import jax.numpy as jnp
from jax import lax
from jax.experimental import pallas as pl
from jax.experimental.pallas import tpu as pltpu
from jax.sharding import Mesh
from jax.sharding import PartitionSpec as P

CLASS = 12
PAIR = 2
HELD = 8
LANES = 128

DP = ("zh", "zl", "xl", "core")
LON = ("y", "xh")
NEAR = ("zl", "xl", "y", "xh")
TILES = 320


def swap_cores(block):
    return lax.ppermute(block, "core", [(0, 1), (1, 0)])


def exchange(blocks, axes):
    return lax.all_to_all(blocks, axes, 0, 0, tiled=True)


def gather_copies(block, axes):
    peers = lax.axis_size(axes)
    return exchange(jnp.broadcast_to(block[None], (peers,) + block.shape), axes)


def sum_four(own, axis):
    near, far, last = [
        lax.ppermute(own, axis, [(i, i ^ m) for i in range(4)]).astype(jnp.float32) for m in (1, 2, 3)
    ]
    return (own.astype(jnp.float32) + near) + (far + last)


def gate_slope(pre_act):
    sigmoid_val = jax.nn.sigmoid(pre_act)
    return sigmoid_val * (1.0 + pre_act * (1.0 - sigmoid_val))


def half_turn(tile):
    return pltpu.roll(tile, 4, 0)


def ends_swapped(tile, top):
    return jnp.where(top, pltpu.roll(tile, 2, 0), pltpu.roll(tile, 6, 0))


def local_body(core_ref, cls_ref, taps_ref, pw_ref, pb_ref, kept_ref, sent_ref, fg_ref, depth, dgr, terms):
    channels, outputs = pw_ref.shape[1:]
    tiles = channels // LANES
    wide = outputs // LANES
    blocks = channels // HELD

    def store_row(branch, row, value):
        tile = blocks * wide + row // HELD
        at = row % HELD
        terms[branch, tile // wide, tile % wide, at : at + 1, :] = value

    sub = lax.broadcasted_iota(jnp.int32, (HELD, LANES), 0)
    top = sub < 4
    first = sub < 2
    end = sub >= 6

    def tap(branch, a, e, lanes):
        row = branch * 9 + (a + 1) * 3 + e + 1
        return jnp.broadcast_to(taps_ref[row : row + 1, lanes], (HELD, LANES))

    def ends(up, down):
        return jnp.where(first, up, jnp.where(end, down, 0.0))

    def both(branch, a, lanes):
        return tap(branch, a, -1, lanes) + tap(branch, a, 1, lanes)

    def read(ref, step, lanes, branch=None):
        out = []
        for k in range(6):
            rows = pl.ds(pl.multiple_of(k * 96 + step * 16, 16), 16)
            tile = (ref[rows, lanes] if branch is None else ref[branch, rows, lanes]).astype(jnp.float32)
            out.append((tile[:HELD], tile[HELD:]))
        return [[pair[h] for pair in out] for h in range(2)]

    for t in range(tiles):
        lanes = slice(t * LANES, (t + 1) * LANES)
        mid_a = [tap(0, 0, e, lanes) for e in (-1, 0, 1)]
        off_a = [jnp.where(top, tap(0, 1, e, lanes), tap(0, -1, e, lanes)) for e in (-1, 0, 1)]
        mid_b = [tap(1, 0, 0, lanes), both(1, 0, lanes)]
        off_b = [
            ends(tap(1, 1, 0, lanes), tap(1, -1, 0, lanes)),
            ends(both(1, 1, lanes), both(1, -1, lanes)),
        ]

        def forward(step, carry):
            made_a, made_b = [], []
            for xs in read(cls_ref, step, lanes):
                turned = [half_turn(x) for x in xs]
                swapped = [ends_swapped(x, top) for x in xs]
                made_a.append(
                    [
                        sum(
                            mid_a[n] * xs[(k + 2 * n - 2) % 6] + off_a[n] * turned[(k + 2 * n - 2) % 6]
                            for n in range(3)
                        )
                        for k in range(6)
                    ]
                )
                made_b.append(
                    [
                        mid_b[0] * xs[k]
                        + mid_b[1] * xs[(k + 3) % 6]
                        + off_b[0] * swapped[k]
                        + off_b[1] * swapped[(k + 3) % 6]
                        for k in range(6)
                    ]
                )
            for k in range(6):
                rows = pl.ds(pl.multiple_of(k * 96 + step * 16, 16), 16)
                for branch, made in enumerate((made_a, made_b)):
                    tile = jnp.concatenate([made[0][k], made[1][k]], axis=0)
                    depth[branch, rows, lanes] = tile.astype(jnp.bfloat16)
            return carry

        lax.fori_loop(0, 6, forward, 0)

    for branch in range(2):
        act = jnp.dot(depth[branch], pw_ref[branch], preferred_element_type=jnp.float32)
        act = act + pb_ref[branch : branch + 1, :]
        start = channels + branch * outputs
        up = cls_ref[:, start : start + outputs].astype(jnp.float32)
        pgrad = (up * gate_slope(act)).astype(jnp.bfloat16)
        point = lax.dot_general(
            depth[branch], pgrad, (((0,), (0,)), ((), ())), preferred_element_type=jnp.float32
        )
        point = point.reshape(blocks, HELD, outputs)
        bias = jnp.sum(pgrad.astype(jnp.float32), axis=0, keepdims=True)
        rest = terms.shape[1] - blocks
        terms[branch, blocks:] = jnp.zeros((rest, wide, HELD, LANES), jnp.float32)
        for h in range(wide):
            lanes = slice(h * LANES, (h + 1) * LANES)
            terms[branch, :blocks, h] = point[:, :, lanes]
            store_row(branch, 9 * tiles + h, bias[:, lanes])
        for c in range(0, channels, 384):
            part = lax.dot_general(
                pgrad, pw_ref[branch, c : c + 384, :], (((1,), (1,)), ((), ())), preferred_element_type=jnp.float32
            )
            dgr[branch, :, c : c + 384] = part.astype(jnp.bfloat16)

    for t in range(tiles):
        lanes = slice(t * LANES, (t + 1) * LANES)
        mid_a = [tap(0, 0, e, lanes) for e in (-1, 0, 1)]
        off_a = [jnp.where(top, tap(0, -1, e, lanes), tap(0, 1, e, lanes)) for e in (-1, 0, 1)]
        mid_b = [tap(1, 0, 0, lanes), both(1, 0, lanes)]
        off_b = [
            ends(tap(1, -1, 0, lanes), tap(1, 1, 0, lanes)),
            ends(both(1, -1, lanes), both(1, 1, lanes)),
        ]

        def backward(step, sums):
            sums = list(sums)
            made = []
            sides = zip(read(cls_ref, step, lanes), read(dgr, step, lanes, 0), read(dgr, step, lanes, 1))
            for xs, das, dbs in sides:
                turned = [half_turn(d) for d in das]
                swapped = [ends_swapped(d, top) for d in dbs]
                made.append(
                    [
                        sum(
                            mid_a[n] * das[(k - 2 * n + 2) % 6] + off_a[n] * turned[(k - 2 * n + 2) % 6]
                            for n in range(3)
                        )
                        + mid_b[0] * dbs[k]
                        + mid_b[1] * dbs[(k + 3) % 6]
                        + off_b[0] * swapped[k]
                        + off_b[1] * swapped[(k + 3) % 6]
                        for k in range(6)
                    ]
                )
                for n in range(3):
                    sums[n] += sum(xs[(k + 2 * n - 2) % 6] * das[k] for k in range(6))
                    sums[3 + n] += sum(xs[(k + 2 * n - 2) % 6] * turned[k] for k in range(6))
                for n in range(2):
                    sums[6 + n] += sum(xs[(k + 3 * n) % 6] * dbs[k] for k in range(6))
                    sums[8 + n] += sum(xs[(k + 3 * n) % 6] * swapped[k] for k in range(6))
            for k in range(6):
                rows = pl.ds(pl.multiple_of(k * 96 + step * 16, 16), 16)
                fg_ref[rows, lanes] = jnp.concatenate([made[0][k], made[1][k]], axis=0).astype(jnp.bfloat16)
            return tuple(sums)

        sums = lax.fori_loop(0, 6, backward, tuple(jnp.zeros((HELD, LANES), jnp.float32) for _ in range(10)))

        def keep(branch, a, e, value, mask=None):
            value = value if mask is None else jnp.where(mask, value, 0.0)
            row = ((a + 1) * 3 + e + 1) * tiles + t
            store_row(branch, row, jnp.sum(value, axis=0, keepdims=True))

        for n in range(3):
            keep(0, 0, n - 1, sums[n])
            keep(0, 1, n - 1, sums[3 + n], jnp.logical_not(top))
            keep(0, -1, n - 1, sums[3 + n], top)
        for e in (-1, 0, 1):
            keep(1, 0, e, sums[6 + abs(e)])
            keep(1, 1, e, sums[8 + abs(e)], end)
            keep(1, -1, e, sums[8 + abs(e)], first)

    @pl.when(core_ref[0] == 0)
    def _():
        kept_ref[...] = terms[0]
        sent_ref[...] = terms[1].astype(jnp.bfloat16)

    @pl.when(core_ref[0] != 0)
    def _():
        kept_ref[...] = terms[1]
        sent_ref[...] = terms[0].astype(jnp.bfloat16)


def local_work(core, field, taps, point_w, point_bias):
    cells = field.shape[0]
    branches, channels, outputs = point_w.shape
    wide = outputs // LANES
    packed = (TILES // wide, wide, HELD, LANES)
    vmem = pl.BlockSpec(memory_space=pltpu.VMEM)
    return pl.pallas_call(
        local_body,
        out_shape=(
            jax.ShapeDtypeStruct(packed, jnp.float32),
            jax.ShapeDtypeStruct(packed, jnp.bfloat16),
            jax.ShapeDtypeStruct((cells, channels), jnp.bfloat16),
        ),
        in_specs=[pl.BlockSpec(memory_space=pltpu.SMEM)] + [vmem] * 4,
        out_specs=(vmem, vmem, vmem),
        scratch_shapes=[
            pltpu.VMEM((branches, cells, channels), jnp.bfloat16),
            pltpu.VMEM((branches, cells, channels), jnp.bfloat16),
            pltpu.VMEM((branches,) + packed, jnp.float32),
        ],
        compiler_params=pltpu.CompilerParams(vmem_limit_bytes=48 << 20),
        name="local_work",
    )(core, field, taps, point_w, point_bias)


def to_chunks(field):
    _, columns, rows, width = field.shape
    groups = CLASS // PAIR
    chunks = field.reshape(columns, rows // CLASS, groups, PAIR, width).transpose(2, 0, 1, 3, 4)
    return chunks.reshape(groups, columns, rows // groups, width)


def per_device(features, depth_w, point_w, point_bias, cotangent):
    _, columns, rows, channels = features.shape
    branches, _, outputs = point_w.shape
    images = lax.axis_size(DP) * features.shape[0]
    peers = lax.axis_size(LON)
    near = lax.axis_size(NEAR)
    groups = CLASS // PAIR
    core = lax.axis_index("core")

    chunks = jnp.concatenate([to_chunks(features), to_chunks(cotangent)], axis=3)
    chunks = jnp.pad(chunks, ((0, peers - groups), (0, 0), (0, 0), (0, 0)))
    field = exchange(chunks, LON).reshape(peers * columns * HELD, chunks.shape[3])
    taps = depth_w.astype(jnp.float32).reshape(branches * 9, channels)
    kept, sent, fgrad = local_work(core.reshape(1), field, taps, point_w, point_bias)

    terms = (kept + swap_cores(sent).astype(jnp.float32)).astype(jnp.bfloat16)
    terms = exchange(terms.reshape(near, -1, LANES), NEAR)
    fgrad, terms = lax.optimization_barrier((fgrad, terms))
    fgrad = exchange(fgrad.reshape(peers, columns, HELD, channels), LON)
    terms = jnp.sum(terms.astype(jnp.float32), axis=0)
    total = (sum_four(terms, "zh") / images).astype(jnp.bfloat16)
    fgrad, total = lax.optimization_barrier((fgrad, total))
    total = gather_copies(total, NEAR).reshape(-1, LANES)
    other = swap_cores(total)
    total = jnp.stack([jnp.where(core == 0, total, other), jnp.where(core == 0, other, total)])

    main = channels * outputs // LANES
    point_grad = total[:, :main].reshape(branches, channels // HELD, outputs // LANES, HELD, LANES)
    point_grad = point_grad.transpose(0, 1, 3, 2, 4).reshape(point_w.shape)
    last = main + 9 * channels // LANES
    depth_grad = total[:, main:last].reshape(depth_w.shape)
    bias_grad = total[:, last : last + outputs // LANES].reshape(branches, outputs).astype(jnp.float32)
    fgrad = fgrad[:groups].reshape(groups, columns, rows // CLASS, PAIR, channels)
    feature_grad = fgrad.transpose(1, 2, 0, 3, 4).reshape(features.shape)
    return (feature_grad, depth_grad, point_grad, bias_grad)


def solution(mesh):
    fine = Mesh(mesh.devices.reshape(4, 4, 2, 2, 4, 2), DP + LON)
    placed = (P(DP, LON, None, None), P(), P(), P(), P(DP, LON, None, None))
    return jax.shard_map(
        per_device,
        mesh=fine,
        in_specs=placed,
        out_specs=(P(DP, LON, None, None), P(), P(), P()),
        check_vma=False,
    )
```

```python
import jax
import jax.numpy as jnp
from jax import lax
from jax.experimental import pallas as pl
from jax.experimental.pallas import tpu as pltpu
from jax.sharding import Mesh
from jax.sharding import PartitionSpec as P

CLASS = 12
PAIR = 2
HELD = 8
LANES = 128

DP = ("zh", "zl", "xl", "core")
LON = ("y", "xh")
PLANE = ("xl", "y", "xh")


def swap_cores(block):
    return lax.ppermute(block, "core", [(0, 1), (1, 0)])


def exchange(blocks, axes):
    return lax.all_to_all(blocks, axes, 0, 0, tiled=True)


def gather_copies(block, axes):
    peers = lax.axis_size(axes)
    return exchange(jnp.broadcast_to(block[None], (peers,) + block.shape), axes)


def sum_pair(own, axis, apart):
    pairs = [(i, i ^ apart) for i in range(lax.axis_size(axis))]
    return own.astype(jnp.float32) + lax.ppermute(own, axis, pairs).astype(jnp.float32)


def gate_slope(pre_act):
    sigmoid_val = jax.nn.sigmoid(pre_act)
    return sigmoid_val * (1.0 + pre_act * (1.0 - sigmoid_val))


def half_turn(tile):
    return pltpu.roll(tile, 4, 0)


def ends_swapped(tile, top):
    return jnp.where(top, pltpu.roll(tile, 2, 0), pltpu.roll(tile, 6, 0))


def shard_row(row, main, extra):
    return (row // extra) * (main + extra) + main + row % extra


def local_body(core_ref, cls_ref, taps_ref, pw_ref, pb_ref, kept_ref, sent_ref, fg_ref, depth, dgr, terms):
    channels, outputs = pw_ref.shape[1:]
    shard = terms.shape[1] // 16
    main = channels // 16
    extra = shard - main
    tiles = channels // LANES
    wide = outputs // LANES
    per_tap = -(-tiles // wide)
    sub = lax.broadcasted_iota(jnp.int32, (HELD, LANES), 0)
    top = sub < 4
    first = sub < 2
    end = sub >= 6

    def tap(branch, a, e, lanes):
        row = branch * 9 + (a + 1) * 3 + e + 1
        return jnp.broadcast_to(taps_ref[row : row + 1, lanes], (HELD, LANES))

    def ends(up, down):
        return jnp.where(first, up, jnp.where(end, down, 0.0))

    def both(branch, a, lanes):
        return tap(branch, a, -1, lanes) + tap(branch, a, 1, lanes)

    def read(ref, step, lanes, branch=None):
        out = []
        for k in range(6):
            rows = pl.ds(pl.multiple_of(k * 96 + step * 16, 16), 16)
            tile = (ref[rows, lanes] if branch is None else ref[branch, rows, lanes]).astype(jnp.float32)
            out.append((tile[:HELD], tile[HELD:]))
        return [[pair[h] for pair in out] for h in range(2)]

    for t in range(tiles):
        lanes = slice(t * LANES, (t + 1) * LANES)
        mid_a = [tap(0, 0, e, lanes) for e in (-1, 0, 1)]
        off_a = [jnp.where(top, tap(0, 1, e, lanes), tap(0, -1, e, lanes)) for e in (-1, 0, 1)]
        mid_b = [tap(1, 0, 0, lanes), both(1, 0, lanes)]
        off_b = [
            ends(tap(1, 1, 0, lanes), tap(1, -1, 0, lanes)),
            ends(both(1, 1, lanes), both(1, -1, lanes)),
        ]

        def forward(step, carry):
            made_a, made_b = [], []
            for xs in read(cls_ref, step, lanes):
                turned = [half_turn(x) for x in xs]
                swapped = [ends_swapped(x, top) for x in xs]
                made_a.append(
                    [
                        sum(
                            mid_a[n] * xs[(k + 2 * n - 2) % 6] + off_a[n] * turned[(k + 2 * n - 2) % 6]
                            for n in range(3)
                        )
                        for k in range(6)
                    ]
                )
                made_b.append(
                    [
                        mid_b[0] * xs[k]
                        + mid_b[1] * xs[(k + 3) % 6]
                        + off_b[0] * swapped[k]
                        + off_b[1] * swapped[(k + 3) % 6]
                        for k in range(6)
                    ]
                )
            for k in range(6):
                rows = pl.ds(pl.multiple_of(k * 96 + step * 16, 16), 16)
                for branch, made in enumerate((made_a, made_b)):
                    tile = jnp.concatenate([made[0][k], made[1][k]], axis=0)
                    depth[branch, rows, lanes] = tile.astype(jnp.bfloat16)
            return carry

        lax.fori_loop(0, 6, forward, 0)

    for branch in range(2):
        act = jnp.dot(depth[branch], pw_ref[branch], preferred_element_type=jnp.float32)
        act = act + pb_ref[branch : branch + 1, :]
        start = channels + branch * outputs
        up = cls_ref[:, start : start + outputs].astype(jnp.float32)
        pgrad = (up * gate_slope(act)).astype(jnp.bfloat16)
        point = lax.dot_general(
            depth[branch], pgrad, (((0,), (0,)), ((), ())), preferred_element_type=jnp.float32
        )
        for p in range(16):
            terms[branch, p * shard : p * shard + main, :] = point[p * main : (p + 1) * main]
            terms[branch, p * shard + main : (p + 1) * shard, :] = jnp.zeros((extra, outputs), jnp.float32)
        row = shard_row(9 * per_tap, main, extra)
        terms[branch, row : row + 1, :] = jnp.sum(pgrad.astype(jnp.float32), axis=0, keepdims=True)
        for c in range(0, channels, 384):
            part = lax.dot_general(
                pgrad, pw_ref[branch, c : c + 384, :], (((1,), (1,)), ((), ())), preferred_element_type=jnp.float32
            )
            dgr[branch, :, c : c + 384] = part.astype(jnp.bfloat16)

    for t in range(tiles):
        lanes = slice(t * LANES, (t + 1) * LANES)
        mid_a = [tap(0, 0, e, lanes) for e in (-1, 0, 1)]
        off_a = [jnp.where(top, tap(0, -1, e, lanes), tap(0, 1, e, lanes)) for e in (-1, 0, 1)]
        mid_b = [tap(1, 0, 0, lanes), both(1, 0, lanes)]
        off_b = [
            ends(tap(1, -1, 0, lanes), tap(1, 1, 0, lanes)),
            ends(both(1, -1, lanes), both(1, 1, lanes)),
        ]

        def backward(step, sums):
            sums = list(sums)
            made = []
            sides = zip(read(cls_ref, step, lanes), read(dgr, step, lanes, 0), read(dgr, step, lanes, 1))
            for xs, das, dbs in sides:
                turned = [half_turn(d) for d in das]
                swapped = [ends_swapped(d, top) for d in dbs]
                made.append(
                    [
                        sum(
                            mid_a[n] * das[(k - 2 * n + 2) % 6] + off_a[n] * turned[(k - 2 * n + 2) % 6]
                            for n in range(3)
                        )
                        + mid_b[0] * dbs[k]
                        + mid_b[1] * dbs[(k + 3) % 6]
                        + off_b[0] * swapped[k]
                        + off_b[1] * swapped[(k + 3) % 6]
                        for k in range(6)
                    ]
                )
                for n in range(3):
                    sums[n] += sum(xs[(k + 2 * n - 2) % 6] * das[k] for k in range(6))
                    sums[3 + n] += sum(xs[(k + 2 * n - 2) % 6] * turned[k] for k in range(6))
                for n in range(2):
                    sums[6 + n] += sum(xs[(k + 3 * n) % 6] * dbs[k] for k in range(6))
                    sums[8 + n] += sum(xs[(k + 3 * n) % 6] * swapped[k] for k in range(6))
            for k in range(6):
                rows = pl.ds(pl.multiple_of(k * 96 + step * 16, 16), 16)
                fg_ref[rows, lanes] = jnp.concatenate([made[0][k], made[1][k]], axis=0).astype(jnp.bfloat16)
            return tuple(sums)

        sums = lax.fori_loop(0, 6, backward, tuple(jnp.zeros((HELD, LANES), jnp.float32) for _ in range(10)))

        def keep(branch, a, e, value, mask=None):
            value = value if mask is None else jnp.where(mask, value, 0.0)
            row = shard_row(((a + 1) * 3 + e + 1) * per_tap + t // wide, main, extra)
            at = (t % wide) * LANES
            terms[branch, row : row + 1, at : at + LANES] = jnp.sum(value, axis=0, keepdims=True)

        for n in range(3):
            keep(0, 0, n - 1, sums[n])
            keep(0, 1, n - 1, sums[3 + n], jnp.logical_not(top))
            keep(0, -1, n - 1, sums[3 + n], top)
        for e in (-1, 0, 1):
            keep(1, 0, e, sums[6 + abs(e)])
            keep(1, 1, e, sums[8 + abs(e)], end)
            keep(1, -1, e, sums[8 + abs(e)], first)

    @pl.when(core_ref[0] == 0)
    def _():
        kept_ref[...] = terms[0]
        sent_ref[...] = terms[1].astype(jnp.bfloat16)

    @pl.when(core_ref[0] != 0)
    def _():
        kept_ref[...] = terms[1]
        sent_ref[...] = terms[0].astype(jnp.bfloat16)


def local_work(core, field, taps, point_w, point_bias):
    cells = field.shape[0]
    branches, channels, outputs = point_w.shape
    rows = 16 * (channels // 16 + 8)
    vmem = pl.BlockSpec(memory_space=pltpu.VMEM)
    return pl.pallas_call(
        local_body,
        out_shape=(
            jax.ShapeDtypeStruct((rows, outputs), jnp.float32),
            jax.ShapeDtypeStruct((rows, outputs), jnp.bfloat16),
            jax.ShapeDtypeStruct((cells, channels), jnp.bfloat16),
        ),
        in_specs=[pl.BlockSpec(memory_space=pltpu.SMEM)] + [vmem] * 4,
        out_specs=(vmem, vmem, vmem),
        scratch_shapes=[
            pltpu.VMEM((branches, cells, channels), jnp.bfloat16),
            pltpu.VMEM((branches, cells, channels), jnp.bfloat16),
            pltpu.VMEM((branches, rows, outputs), jnp.float32),
        ],
        compiler_params=pltpu.CompilerParams(vmem_limit_bytes=48 << 20),
        name="local_work",
    )(core, field, taps, point_w, point_bias)


def to_chunks(field):
    _, columns, rows, width = field.shape
    groups = CLASS // PAIR
    chunks = field.reshape(columns, rows // CLASS, groups, PAIR, width).transpose(2, 0, 1, 3, 4)
    return chunks.reshape(groups, columns, rows // groups, width)


def per_device(features, depth_w, point_w, point_bias, cotangent):
    _, columns, rows, channels = features.shape
    branches, _, outputs = point_w.shape
    images = lax.axis_size(DP) * features.shape[0]
    peers = lax.axis_size(LON)
    plane = lax.axis_size(PLANE)
    groups = CLASS // PAIR
    core = lax.axis_index("core")

    chunks = jnp.concatenate([to_chunks(features), to_chunks(cotangent)], axis=3)
    chunks = jnp.pad(chunks, ((0, peers - groups), (0, 0), (0, 0), (0, 0)))
    field = exchange(chunks, LON).reshape(peers * columns * HELD, chunks.shape[3])
    taps = depth_w.astype(jnp.float32).reshape(branches * 9, channels)
    kept, sent, fgrad = local_work(core.reshape(1), field, taps, point_w, point_bias)

    terms = (kept + swap_cores(sent).astype(jnp.float32)).astype(jnp.bfloat16)
    shard = terms.shape[0] // plane
    terms = exchange(terms.reshape(plane, shard, outputs), PLANE)
    fgrad, terms = lax.optimization_barrier((fgrad, terms))
    fgrad = exchange(fgrad.reshape(peers, columns, HELD, channels), LON)
    terms = jnp.sum(terms.astype(jnp.float32), axis=0)
    terms = sum_pair(sum_pair(terms, "zl", 1), "zl", 2)
    terms = sum_pair(terms.astype(jnp.bfloat16), "zh", 1)
    terms = sum_pair(terms.astype(jnp.bfloat16), "zh", 2)
    total = (terms / images).astype(jnp.bfloat16)
    fgrad, total = lax.optimization_barrier((fgrad, total))
    total = gather_copies(total, PLANE)
    fgrad = fgrad[:groups].reshape(groups, columns, rows // CLASS, PAIR, channels)
    feature_grad = fgrad.transpose(1, 2, 0, 3, 4).reshape(features.shape)
    feature_grad, total = lax.optimization_barrier((feature_grad, total))
    other = swap_cores(total)
    total = jnp.stack([jnp.where(core == 0, total, other), jnp.where(core == 0, other, total)])

    main = channels // plane
    point_grad = total[:, :, :main].reshape(point_w.shape)
    small = total[:, :, main:].reshape(branches, -1, outputs)
    per_tap = -(-channels // outputs)
    depth_grad = small[:, : 9 * per_tap].reshape(branches, 9, -1)[:, :, :channels].reshape(depth_w.shape)
    bias_grad = small[:, 9 * per_tap].astype(jnp.float32)
    return (feature_grad, depth_grad, point_grad, bias_grad)


def solution(mesh):
    fine = Mesh(mesh.devices.reshape(4, 4, 2, 2, 4, 2), DP + LON)
    placed = (P(DP, LON, None, None), P(), P(), P(), P(DP, LON, None, None))
    return jax.shard_map(
        per_device,
        mesh=fine,
        in_specs=placed,
        out_specs=(P(DP, LON, None, None), P(), P(), P()),
        check_vma=False,
    )
```

```python
import jax
import jax.numpy as jnp
import numpy as np
from jax import lax
from jax.experimental import pallas as pl
from jax.experimental.pallas import tpu as pltpu
from jax.sharding import Mesh
from jax.sharding import PartitionSpec as P

CLASS = 12
PAIRS = 6
PEERS = 8
SLOTS = 7
HELD = 8
LANES = 128

DP = ("zh", "zl", "xl", "core")
LON = ("y", "xh")
PLANE = ("xl", "y", "xh")


def swap_cores(block):
    return lax.ppermute(block, "core", [(0, 1), (1, 0)])


def exchange(blocks, axes):
    return lax.all_to_all(blocks, axes, 0, 0, tiled=True)


def gather_copies(block, axes):
    peers = lax.axis_size(axes)
    return exchange(jnp.broadcast_to(block[None], (peers,) + block.shape), axes)


def sum_pair(own, axis, apart):
    pairs = [(i, i ^ apart) for i in range(lax.axis_size(axis))]
    return own.astype(jnp.float32) + lax.ppermute(own, axis, pairs).astype(jnp.float32)


def deal_units(columns):
    blocks = CLASS // 3
    owned = [[] for _ in range(PEERS)]
    for m in range(blocks):
        units = iter([(c, q) for q in range(PAIRS) for c in range(3 * m, 3 * m + 3)])
        for e in range(PEERS):
            owned[e] += [next(units) for _ in range(2 + (e % blocks == m))]
    home = np.zeros((PEERS, columns * PAIRS), np.int32)
    away = np.zeros((PEERS, columns * PAIRS), np.int32)
    used = np.zeros((PEERS, PEERS), np.int32)
    for e in range(PEERS):
        for u, (c, q) in enumerate(owned[e]):
            for k in range(6):
                d, j = divmod(c + CLASS * k, columns)
                home[d, j * PAIRS + q] = e * SLOTS + used[d, e]
                away[e, u * 6 + k] = d * SLOTS + used[d, e]
                used[d, e] += 1
    assert used.max() == SLOTS and used.min() == SLOTS - 1
    return home.reshape(-1), away.reshape(-1)


def blank_slots(ref, lon):
    for block in (3 - lon % 4, 7 - lon % 4):
        ref[block * SLOTS + SLOTS - 1] = jnp.zeros(ref.shape[1:], ref.dtype)


def pack_body(who_ref, home_ref, feat_ref, cot_ref, out_ref):
    columns, _, channels = feat_ref.shape
    lon = who_ref[0]
    blank_slots(out_ref, lon)

    def column(j, carry):
        for source, start in ((feat_ref, 0), (cot_ref, channels)):
            width = source.shape[2]
            rows = source[j].astype(jnp.float32)
            for q in range(PAIRS):
                slot = home_ref[(lon * columns + j) * PAIRS + q]
                tile = jnp.concatenate([rows[12 * n + 2 * q : 12 * n + 2 * q + 2] for n in range(4)], axis=0)
                out_ref[slot, :, start : start + width] = tile.astype(out_ref.dtype)
        return carry

    lax.fori_loop(0, columns, column, 0)


def unpack_body(who_ref, home_ref, tiles_ref, out_ref):
    columns = out_ref.shape[0]
    lon = who_ref[0]

    def column(j, carry):
        tiles = [tiles_ref[home_ref[(lon * columns + j) * PAIRS + q]].astype(jnp.float32) for q in range(PAIRS)]
        rows = [tiles[q][2 * n : 2 * n + 2] for n in range(4) for q in range(PAIRS)]
        out_ref[j] = jnp.concatenate(rows, axis=0).astype(out_ref.dtype)
        return carry

    lax.fori_loop(0, columns, column, 0)


def on_chip(body, out_shape, scalars, arrays, scratch=(), name=None):
    vmem = pl.BlockSpec(memory_space=pltpu.VMEM)
    smem = pl.BlockSpec(memory_space=pltpu.SMEM)
    return pl.pallas_call(
        body,
        out_shape=out_shape,
        in_specs=[smem] * len(scalars) + [vmem] * len(arrays),
        out_specs=jax.tree.map(lambda _: vmem, out_shape),
        scratch_shapes=list(scratch),
        compiler_params=pltpu.CompilerParams(vmem_limit_bytes=48 << 20),
        name=name,
    )(*scalars, *arrays)


def gate_slope(pre_act):
    sigmoid_val = jax.nn.sigmoid(pre_act)
    return sigmoid_val * (1.0 + pre_act * (1.0 - sigmoid_val))


def half_turn(tile):
    return pltpu.roll(tile, 4, 0)


def ends_swapped(tile, top):
    return jnp.where(top, pltpu.roll(tile, 2, 0), pltpu.roll(tile, 6, 0))


def shard_row(row, main, extra):
    return (row // extra) * (main + extra) + main + row % extra


def local_body(
    who_ref, core_ref, away_ref, cls_ref, taps_ref, pw_ref, pb_ref, kept_ref, sent_ref, fg_ref, depth, dgr, upstream, terms
):
    channels, outputs = pw_ref.shape[1:]
    shard = terms.shape[1] // 16
    main = channels // 16
    extra = shard - main
    tiles = channels // LANES
    wide = outputs // LANES
    per_tap = -(-tiles // wide)
    sub = lax.broadcasted_iota(jnp.int32, (HELD, LANES), 0)
    top = sub < 4
    first = sub < 2
    end = sub >= 6

    def tap(branch, a, e, lanes):
        row = branch * 9 + (a + 1) * 3 + e + 1
        return jnp.broadcast_to(taps_ref[row : row + 1, lanes], (HELD, LANES))

    def ends(up, down):
        return jnp.where(first, up, jnp.where(end, down, 0.0))

    def both(branch, a, lanes):
        return tap(branch, a, -1, lanes) + tap(branch, a, 1, lanes)

    units = depth.shape[1] // (6 * HELD)
    lon = who_ref[0]
    blank_slots(fg_ref, lon)

    def slots(u):
        return [away_ref[(lon * units + u) * 6 + k] for k in range(6)]

    def pair_rows(u, k):
        return pl.ds(pl.multiple_of((u * 6 + k) * HELD, 16), 16)

    def read_pairs(ref, branch, u, lanes):
        out = []
        for k in range(0, 6, 2):
            pair = ref[branch, pair_rows(u, k), lanes].astype(jnp.float32)
            out += [pair[:HELD], pair[HELD:]]
        return out

    def write_pairs(ref, branch, u, lanes, made):
        for k in range(0, 6, 2):
            pair = jnp.concatenate([made[k], made[k + 1]], axis=0)
            ref[branch, pair_rows(u, k), lanes] = pair.astype(jnp.bfloat16)

    def gather_upstream(u, carry):
        at = slots(u)
        for k in range(0, 6, 2):
            for c in range(channels, cls_ref.shape[2], LANES):
                lanes = slice(c, c + LANES)
                pair = jnp.concatenate([cls_ref[at[k + n], :, lanes].astype(jnp.float32) for n in range(2)], axis=0)
                upstream[pair_rows(u, k), c - channels : c - channels + LANES] = pair
        return carry

    lax.fori_loop(0, units, gather_upstream, 0)

    for t in range(tiles):
        lanes = slice(t * LANES, (t + 1) * LANES)
        mid_a = [tap(0, 0, e, lanes) for e in (-1, 0, 1)]
        off_a = [jnp.where(top, tap(0, 1, e, lanes), tap(0, -1, e, lanes)) for e in (-1, 0, 1)]
        mid_b = [tap(1, 0, 0, lanes), both(1, 0, lanes)]
        off_b = [
            ends(tap(1, 1, 0, lanes), tap(1, -1, 0, lanes)),
            ends(both(1, 1, lanes), both(1, -1, lanes)),
        ]

        def forward(u, carry):
            xs = [cls_ref[slot, :, lanes].astype(jnp.float32) for slot in slots(u)]
            turned = [half_turn(x) for x in xs]
            swapped = [ends_swapped(x, top) for x in xs]
            made_a = [
                sum(
                    mid_a[n] * xs[(k + 2 * n - 2) % 6] + off_a[n] * turned[(k + 2 * n - 2) % 6] for n in range(3)
                )
                for k in range(6)
            ]
            made_b = [
                mid_b[0] * xs[k]
                + mid_b[1] * xs[(k + 3) % 6]
                + off_b[0] * swapped[k]
                + off_b[1] * swapped[(k + 3) % 6]
                for k in range(6)
            ]
            write_pairs(depth, 0, u, lanes, made_a)
            write_pairs(depth, 1, u, lanes, made_b)
            return carry

        lax.fori_loop(0, units, forward, 0)

    for branch in range(2):
        act = jnp.dot(depth[branch], pw_ref[branch], preferred_element_type=jnp.float32)
        act = act + pb_ref[branch : branch + 1, :]
        up = upstream[:, branch * outputs : (branch + 1) * outputs]
        pgrad = (up * gate_slope(act)).astype(jnp.bfloat16)
        point = lax.dot_general(
            depth[branch], pgrad, (((0,), (0,)), ((), ())), preferred_element_type=jnp.float32
        )
        for p in range(16):
            terms[branch, p * shard : p * shard + main, :] = point[p * main : (p + 1) * main]
            terms[branch, p * shard + main : (p + 1) * shard, :] = jnp.zeros((extra, outputs), jnp.float32)
        row = shard_row(9 * per_tap, main, extra)
        terms[branch, row : row + 1, :] = jnp.sum(pgrad.astype(jnp.float32), axis=0, keepdims=True)
        for c in range(0, channels, 384):
            part = lax.dot_general(
                pgrad, pw_ref[branch, c : c + 384, :], (((1,), (1,)), ((), ())), preferred_element_type=jnp.float32
            )
            dgr[branch, :, c : c + 384] = part.astype(jnp.bfloat16)

    for t in range(tiles):
        lanes = slice(t * LANES, (t + 1) * LANES)
        mid_a = [tap(0, 0, e, lanes) for e in (-1, 0, 1)]
        off_a = [jnp.where(top, tap(0, -1, e, lanes), tap(0, 1, e, lanes)) for e in (-1, 0, 1)]
        mid_b = [tap(1, 0, 0, lanes), both(1, 0, lanes)]
        off_b = [
            ends(tap(1, -1, 0, lanes), tap(1, 1, 0, lanes)),
            ends(both(1, -1, lanes), both(1, 1, lanes)),
        ]

        def backward(u, sums):
            sums = list(sums)
            at = slots(u)
            xs = [cls_ref[slot, :, lanes].astype(jnp.float32) for slot in at]
            das = read_pairs(dgr, 0, u, lanes)
            dbs = read_pairs(dgr, 1, u, lanes)
            turned = [half_turn(d) for d in das]
            swapped = [ends_swapped(d, top) for d in dbs]
            for k in range(6):
                made = (
                    sum(
                        mid_a[n] * das[(k - 2 * n + 2) % 6] + off_a[n] * turned[(k - 2 * n + 2) % 6]
                        for n in range(3)
                    )
                    + mid_b[0] * dbs[k]
                    + mid_b[1] * dbs[(k + 3) % 6]
                    + off_b[0] * swapped[k]
                    + off_b[1] * swapped[(k + 3) % 6]
                )
                fg_ref[at[k], :, lanes] = made.astype(jnp.bfloat16)
            for n in range(3):
                sums[n] += sum(xs[(k + 2 * n - 2) % 6] * das[k] for k in range(6))
                sums[3 + n] += sum(xs[(k + 2 * n - 2) % 6] * turned[k] for k in range(6))
            for n in range(2):
                sums[6 + n] += sum(xs[(k + 3 * n) % 6] * dbs[k] for k in range(6))
                sums[8 + n] += sum(xs[(k + 3 * n) % 6] * swapped[k] for k in range(6))
            return tuple(sums)

        zero = jnp.zeros((HELD, LANES), jnp.float32)
        sums = lax.fori_loop(0, units, backward, (zero,) * 10)

        def keep(branch, a, e, value, mask=None):
            value = value if mask is None else jnp.where(mask, value, 0.0)
            row = shard_row(((a + 1) * 3 + e + 1) * per_tap + t // wide, main, extra)
            at = (t % wide) * LANES
            terms[branch, row : row + 1, at : at + LANES] = jnp.sum(value, axis=0, keepdims=True)

        for n in range(3):
            keep(0, 0, n - 1, sums[n])
            keep(0, 1, n - 1, sums[3 + n], jnp.logical_not(top))
            keep(0, -1, n - 1, sums[3 + n], top)
        for e in (-1, 0, 1):
            keep(1, 0, e, sums[6 + abs(e)])
            keep(1, 1, e, sums[8 + abs(e)], end)
            keep(1, -1, e, sums[8 + abs(e)], first)

    @pl.when(core_ref[0] == 0)
    def _():
        kept_ref[...] = terms[0]
        sent_ref[...] = terms[1].astype(jnp.bfloat16)

    @pl.when(core_ref[0] != 0)
    def _():
        kept_ref[...] = terms[1]
        sent_ref[...] = terms[0].astype(jnp.bfloat16)


def per_device(features, depth_w, point_w, point_bias, cotangent):
    _, columns, rows, channels = features.shape
    branches, _, outputs = point_w.shape
    images = lax.axis_size(DP) * features.shape[0]
    plane = lax.axis_size(PLANE)
    core = lax.axis_index("core")
    who = lax.axis_index(LON).reshape(1)
    home, away = deal_units(columns)
    cells = columns * rows
    packed_rows = 16 * (channels // 16 + 8)
    width = channels + cotangent.shape[3]
    act = jnp.bfloat16

    packed = on_chip(
        pack_body,
        jax.ShapeDtypeStruct((PEERS * SLOTS, HELD, width), act),
        (who, home),
        (features[0], cotangent[0]),
        name="pack",
    )
    field = exchange(packed.reshape(PEERS, SLOTS, HELD, width), LON).reshape(packed.shape)
    taps = depth_w.astype(jnp.float32).reshape(branches * 9, channels)
    kept, sent, fgrad = on_chip(
        local_body,
        (
            jax.ShapeDtypeStruct((packed_rows, outputs), jnp.float32),
            jax.ShapeDtypeStruct((packed_rows, outputs), act),
            jax.ShapeDtypeStruct((PEERS * SLOTS, HELD, channels), act),
        ),
        (who, core.reshape(1), away),
        (field, taps, point_w, point_bias),
        (
            pltpu.VMEM((branches, cells, channels), act),
            pltpu.VMEM((branches, cells, channels), act),
            pltpu.VMEM((cells, branches * outputs), jnp.float32),
            pltpu.VMEM((branches, packed_rows, outputs), jnp.float32),
        ),
        name="local_work",
    )

    terms = (kept + swap_cores(sent).astype(jnp.float32)).astype(jnp.bfloat16)
    shard = terms.shape[0] // plane
    terms = exchange(terms.reshape(plane, shard, outputs), PLANE)
    fgrad, terms = lax.optimization_barrier((fgrad, terms))
    fgrad = exchange(fgrad.reshape(PEERS, SLOTS, HELD, channels), LON)
    terms = jnp.sum(terms.astype(jnp.float32), axis=0)
    terms = sum_pair(sum_pair(terms, "zl", 1), "zl", 2)
    terms = sum_pair(terms.astype(jnp.bfloat16), "zh", 1)
    terms = sum_pair(terms.astype(jnp.bfloat16), "zh", 2)
    total = (terms / images).astype(jnp.bfloat16)
    fgrad, total = lax.optimization_barrier((fgrad, total))
    total = gather_copies(total, PLANE)
    feature_grad = on_chip(
        unpack_body,
        jax.ShapeDtypeStruct((columns, rows, channels), act),
        (who, home),
        (fgrad.reshape(PEERS * SLOTS, HELD, channels),),
        name="unpack",
    )[None]
    feature_grad, total = lax.optimization_barrier((feature_grad, total))
    other = swap_cores(total)
    total = jnp.stack([jnp.where(core == 0, total, other), jnp.where(core == 0, other, total)])

    main = channels // plane
    point_grad = total[:, :, :main].reshape(point_w.shape)
    small = total[:, :, main:].reshape(branches, -1, outputs)
    per_tap = -(-channels // outputs)
    depth_grad = small[:, : 9 * per_tap].reshape(branches, 9, -1)[:, :, :channels].reshape(depth_w.shape)
    bias_grad = small[:, 9 * per_tap].astype(jnp.float32)
    return (feature_grad, depth_grad, point_grad, bias_grad)


def solution(mesh):
    fine = Mesh(mesh.devices.reshape(4, 4, 2, 2, 4, 2), DP + LON)
    placed = (P(DP, LON, None, None), P(), P(), P(), P(DP, LON, None, None))
    return jax.shard_map(
        per_device,
        mesh=fine,
        in_specs=placed,
        out_specs=(P(DP, LON, None, None), P(), P(), P()),
        check_vma=False,
    )
```

```python
import jax
import jax.numpy as jnp
import numpy as np
from jax import lax
from jax.experimental import pallas as pl
from jax.experimental.pallas import tpu as pltpu
from jax.sharding import Mesh
from jax.sharding import PartitionSpec as P

CLASS = 12
PAIRS = 6
PEERS = 8
SLOTS = 7
HELD = 8
LANES = 128

DP = ("zh", "zl", "xl", "core")
LON = ("y", "xh")
Z = ("zh", "zl")
PLANE = ("xl", "y", "xh")


def swap_cores(block):
    return lax.ppermute(block, "core", [(0, 1), (1, 0)])


def exchange(blocks, axes):
    return lax.all_to_all(blocks, axes, 0, 0, tiled=True)


def gather_copies(block, axes):
    peers = lax.axis_size(axes)
    return exchange(jnp.broadcast_to(block[None], (peers,) + block.shape), axes)


def sum_ring(own, apart):
    planes = lax.axis_size(Z)

    def fetch(block, ahead):
        return lax.ppermute(block, Z, [((i + ahead) % planes, i) for i in range(planes)])

    after = fetch(own, apart)
    before = fetch(own, -apart)
    far = fetch(after, apart)
    own, after, before, far = [x.astype(jnp.float32) for x in (own, after, before, far)]
    return (own + far) + (before + after)


def deal_units(columns):
    blocks = CLASS // 3
    owned = [[] for _ in range(PEERS)]
    for m in range(blocks):
        units = iter([(c, q) for q in range(PAIRS) for c in range(3 * m, 3 * m + 3)])
        for e in range(PEERS):
            owned[e] += [next(units) for _ in range(2 + (e % blocks == m))]
    home = np.zeros((PEERS, columns * PAIRS), np.int32)
    away = np.zeros((PEERS, columns * PAIRS), np.int32)
    used = np.zeros((PEERS, PEERS), np.int32)
    for e in range(PEERS):
        for u, (c, q) in enumerate(owned[e]):
            for k in range(6):
                d, j = divmod(c + CLASS * k, columns)
                home[d, j * PAIRS + q] = e * SLOTS + used[d, e]
                away[e, u * 6 + k] = d * SLOTS + used[d, e]
                used[d, e] += 1
    assert used.max() == SLOTS and used.min() == SLOTS - 1
    return home.reshape(-1), away.reshape(-1)


def blank_slots(ref, lon):
    for block in (3 - lon % 4, 7 - lon % 4):
        ref[block * SLOTS + SLOTS - 1] = jnp.zeros(ref.shape[1:], ref.dtype)


def pack_body(who_ref, home_hbm, feat_hbm, cot_hbm, out_ref, home_ref, feat_ref, cot_ref, table_sem, sems):
    columns, _, channels = feat_ref.shape
    lon = who_ref[0]
    table = pltpu.make_async_copy(home_hbm, home_ref, table_sem)
    table.start()

    def fetch(j):
        return [
            pltpu.make_async_copy(source.at[j], held.at[j], sems.at[n, j])
            for n, (source, held) in enumerate(((feat_hbm, feat_ref), (cot_hbm, cot_ref)))
        ]

    for j in range(columns):
        for copy in fetch(j):
            copy.start()
    blank_slots(out_ref, lon)
    table.wait()

    def column(j, carry):
        for copy in fetch(j):
            copy.wait()
        for source, start in ((feat_ref, 0), (cot_ref, channels)):
            width = source.shape[2]
            rows = source[j].astype(jnp.float32)
            for q in range(PAIRS):
                slot = home_ref[(lon * columns + j) * PAIRS + q]
                tile = jnp.concatenate([rows[12 * n + 2 * q : 12 * n + 2 * q + 2] for n in range(4)], axis=0)
                out_ref[slot, :, start : start + width] = tile.astype(out_ref.dtype)
        return carry

    lax.fori_loop(0, columns, column, 0)


def unpack_body(who_ref, home_ref, tiles_ref, out_ref):
    columns = out_ref.shape[0]
    lon = who_ref[0]

    def column(j, carry):
        tiles = [tiles_ref[home_ref[(lon * columns + j) * PAIRS + q]].astype(jnp.float32) for q in range(PAIRS)]
        rows = [tiles[q][2 * n : 2 * n + 2] for n in range(4) for q in range(PAIRS)]
        out_ref[j] = jnp.concatenate(rows, axis=0).astype(out_ref.dtype)
        return carry

    lax.fori_loop(0, columns, column, 0)


def on_chip(body, out_shape, scalars, arrays, scratch=(), name=None, space=pltpu.VMEM):
    vmem = pl.BlockSpec(memory_space=pltpu.VMEM)
    smem = pl.BlockSpec(memory_space=pltpu.SMEM)
    return pl.pallas_call(
        body,
        out_shape=out_shape,
        in_specs=[smem] * len(scalars) + [pl.BlockSpec(memory_space=space)] * len(arrays),
        out_specs=jax.tree.map(lambda _: vmem, out_shape),
        scratch_shapes=list(scratch),
        compiler_params=pltpu.CompilerParams(vmem_limit_bytes=48 << 20),
        name=name,
    )(*scalars, *arrays)


def gate_slope(pre_act):
    sigmoid_val = jax.nn.sigmoid(pre_act)
    return sigmoid_val * (1.0 + pre_act * (1.0 - sigmoid_val))


def half_turn(tile):
    return pltpu.roll(tile, 4, 0)


def ends_swapped(tile, top):
    return jnp.where(top, pltpu.roll(tile, 2, 0), pltpu.roll(tile, 6, 0))


def shard_row(row, main, extra):
    return (row // extra) * (main + extra) + main + row % extra


def local_body(
    who_ref, core_ref, away_ref, cls_ref, taps_ref, pw_ref, pb_ref, kept_ref, sent_ref, fg_ref, depth, dgr, upstream, terms
):
    channels, outputs = pw_ref.shape[1:]
    shard = terms.shape[1] // 16
    main = channels // 16
    extra = shard - main
    tiles = channels // LANES
    wide = outputs // LANES
    per_tap = -(-tiles // wide)
    sub = lax.broadcasted_iota(jnp.int32, (HELD, LANES), 0)
    top = sub < 4
    first = sub < 2
    end = sub >= 6

    def tap(branch, a, e, lanes):
        row = branch * 9 + (a + 1) * 3 + e + 1
        return jnp.broadcast_to(taps_ref[row : row + 1, lanes], (HELD, LANES))

    def ends(up, down):
        return jnp.where(first, up, jnp.where(end, down, 0.0))

    def both(branch, a, lanes):
        return tap(branch, a, -1, lanes) + tap(branch, a, 1, lanes)

    units = depth.shape[1] // (6 * HELD)
    lon = who_ref[0]
    blank_slots(fg_ref, lon)

    def slots(u):
        return [away_ref[(lon * units + u) * 6 + k] for k in range(6)]

    def pair_rows(u, k):
        return pl.ds(pl.multiple_of((u * 6 + k) * HELD, 16), 16)

    def read_pairs(ref, branch, u, lanes):
        out = []
        for k in range(0, 6, 2):
            pair = ref[branch, pair_rows(u, k), lanes].astype(jnp.float32)
            out += [pair[:HELD], pair[HELD:]]
        return out

    def write_pairs(ref, branch, u, lanes, made):
        for k in range(0, 6, 2):
            pair = jnp.concatenate([made[k], made[k + 1]], axis=0)
            ref[branch, pair_rows(u, k), lanes] = pair.astype(jnp.bfloat16)

    def gather_upstream(u, carry):
        at = slots(u)
        for k in range(0, 6, 2):
            for c in range(channels, cls_ref.shape[2], LANES):
                lanes = slice(c, c + LANES)
                pair = jnp.concatenate([cls_ref[at[k + n], :, lanes].astype(jnp.float32) for n in range(2)], axis=0)
                upstream[pair_rows(u, k), c - channels : c - channels + LANES] = pair
        return carry

    lax.fori_loop(0, units, gather_upstream, 0)

    for t in range(tiles):
        lanes = slice(t * LANES, (t + 1) * LANES)
        mid_a = [tap(0, 0, e, lanes) for e in (-1, 0, 1)]
        off_a = [jnp.where(top, tap(0, 1, e, lanes), tap(0, -1, e, lanes)) for e in (-1, 0, 1)]
        mid_b = [tap(1, 0, 0, lanes), both(1, 0, lanes)]
        off_b = [
            ends(tap(1, 1, 0, lanes), tap(1, -1, 0, lanes)),
            ends(both(1, 1, lanes), both(1, -1, lanes)),
        ]

        def forward(u, carry):
            xs = [cls_ref[slot, :, lanes].astype(jnp.float32) for slot in slots(u)]
            turned = [half_turn(x) for x in xs]
            swapped = [ends_swapped(x, top) for x in xs]
            made_a = [
                sum(
                    mid_a[n] * xs[(k + 2 * n - 2) % 6] + off_a[n] * turned[(k + 2 * n - 2) % 6] for n in range(3)
                )
                for k in range(6)
            ]
            made_b = [
                mid_b[0] * xs[k]
                + mid_b[1] * xs[(k + 3) % 6]
                + off_b[0] * swapped[k]
                + off_b[1] * swapped[(k + 3) % 6]
                for k in range(6)
            ]
            write_pairs(depth, 0, u, lanes, made_a)
            write_pairs(depth, 1, u, lanes, made_b)
            return carry

        lax.fori_loop(0, units, forward, 0, unroll=True)

    for branch in range(2):
        act = jnp.dot(depth[branch], pw_ref[branch], preferred_element_type=jnp.float32)
        act = act + pb_ref[branch : branch + 1, :]
        up = upstream[:, branch * outputs : (branch + 1) * outputs]
        pgrad = (up * gate_slope(act)).astype(jnp.bfloat16)
        point = lax.dot_general(
            depth[branch], pgrad, (((0,), (0,)), ((), ())), preferred_element_type=jnp.float32
        )
        for p in range(16):
            terms[branch, p * shard : p * shard + main, :] = point[p * main : (p + 1) * main]
            terms[branch, p * shard + main : (p + 1) * shard, :] = jnp.zeros((extra, outputs), jnp.float32)
        row = shard_row(9 * per_tap, main, extra)
        terms[branch, row : row + 1, :] = jnp.sum(pgrad.astype(jnp.float32), axis=0, keepdims=True)
        for c in range(0, channels, 384):
            part = lax.dot_general(
                pgrad, pw_ref[branch, c : c + 384, :], (((1,), (1,)), ((), ())), preferred_element_type=jnp.float32
            )
            dgr[branch, :, c : c + 384] = part.astype(jnp.bfloat16)

    for t in range(tiles):
        lanes = slice(t * LANES, (t + 1) * LANES)
        mid_a = [tap(0, 0, e, lanes) for e in (-1, 0, 1)]
        off_a = [jnp.where(top, tap(0, -1, e, lanes), tap(0, 1, e, lanes)) for e in (-1, 0, 1)]
        mid_b = [tap(1, 0, 0, lanes), both(1, 0, lanes)]
        off_b = [
            ends(tap(1, -1, 0, lanes), tap(1, 1, 0, lanes)),
            ends(both(1, -1, lanes), both(1, 1, lanes)),
        ]

        def backward(u, sums):
            sums = list(sums)
            at = slots(u)
            xs = [cls_ref[slot, :, lanes].astype(jnp.float32) for slot in at]
            das = read_pairs(dgr, 0, u, lanes)
            dbs = read_pairs(dgr, 1, u, lanes)
            turned = [half_turn(d) for d in das]
            swapped = [ends_swapped(d, top) for d in dbs]
            for k in range(6):
                made = (
                    sum(
                        mid_a[n] * das[(k - 2 * n + 2) % 6] + off_a[n] * turned[(k - 2 * n + 2) % 6]
                        for n in range(3)
                    )
                    + mid_b[0] * dbs[k]
                    + mid_b[1] * dbs[(k + 3) % 6]
                    + off_b[0] * swapped[k]
                    + off_b[1] * swapped[(k + 3) % 6]
                )
                fg_ref[at[k], :, lanes] = made.astype(jnp.bfloat16)
            for n in range(3):
                sums[n] += sum(xs[(k + 2 * n - 2) % 6] * das[k] for k in range(6))
                sums[3 + n] += sum(xs[(k + 2 * n - 2) % 6] * turned[k] for k in range(6))
            for n in range(2):
                sums[6 + n] += sum(xs[(k + 3 * n) % 6] * dbs[k] for k in range(6))
                sums[8 + n] += sum(xs[(k + 3 * n) % 6] * swapped[k] for k in range(6))
            return tuple(sums)

        zero = jnp.zeros((HELD, LANES), jnp.float32)
        sums = lax.fori_loop(0, units, backward, (zero,) * 10, unroll=True)

        def keep(branch, a, e, value, mask=None):
            value = value if mask is None else jnp.where(mask, value, 0.0)
            row = shard_row(((a + 1) * 3 + e + 1) * per_tap + t // wide, main, extra)
            at = (t % wide) * LANES
            terms[branch, row : row + 1, at : at + LANES] = jnp.sum(value, axis=0, keepdims=True)

        for n in range(3):
            keep(0, 0, n - 1, sums[n])
            keep(0, 1, n - 1, sums[3 + n], jnp.logical_not(top))
            keep(0, -1, n - 1, sums[3 + n], top)
        for e in (-1, 0, 1):
            keep(1, 0, e, sums[6 + abs(e)])
            keep(1, 1, e, sums[8 + abs(e)], end)
            keep(1, -1, e, sums[8 + abs(e)], first)

    @pl.when(core_ref[0] == 0)
    def _():
        kept_ref[...] = terms[0]
        sent_ref[...] = terms[1].astype(jnp.bfloat16)

    @pl.when(core_ref[0] != 0)
    def _():
        kept_ref[...] = terms[1]
        sent_ref[...] = terms[0].astype(jnp.bfloat16)


def per_device(features, depth_w, point_w, point_bias, cotangent):
    _, columns, rows, channels = features.shape
    branches, _, outputs = point_w.shape
    images = lax.axis_size(DP) * features.shape[0]
    plane = lax.axis_size(PLANE)
    core = lax.axis_index("core")
    who = lax.axis_index(LON).reshape(1)
    home, away = deal_units(columns)
    cells = columns * rows
    packed_rows = 16 * (channels // 16 + 8)
    width = channels + cotangent.shape[3]
    act = jnp.bfloat16

    packed = on_chip(
        pack_body,
        jax.ShapeDtypeStruct((PEERS * SLOTS, HELD, width), act),
        (who,),
        [pltpu.with_memory_space_constraint(x, pltpu.HBM) for x in (home, features[0], cotangent[0])],
        (
            pltpu.SMEM(home.shape, jnp.int32),
            pltpu.VMEM((columns, rows, channels), act),
            pltpu.VMEM((columns, rows, cotangent.shape[3]), act),
            pltpu.SemaphoreType.DMA(()),
            pltpu.SemaphoreType.DMA((2, columns)),
        ),
        name="pack",
        space=pltpu.HBM,
    )
    field = exchange(packed.reshape(PEERS, SLOTS, HELD, width), LON).reshape(packed.shape)
    taps = depth_w.astype(jnp.float32).reshape(branches * 9, channels)
    kept, sent, fgrad = on_chip(
        local_body,
        (
            jax.ShapeDtypeStruct((packed_rows, outputs), jnp.float32),
            jax.ShapeDtypeStruct((packed_rows, outputs), act),
            jax.ShapeDtypeStruct((PEERS * SLOTS, HELD, channels), act),
        ),
        (who, core.reshape(1), away),
        (field, taps, point_w, point_bias),
        (
            pltpu.VMEM((branches, cells, channels), act),
            pltpu.VMEM((branches, cells, channels), act),
            pltpu.VMEM((cells, branches * outputs), jnp.float32),
            pltpu.VMEM((branches, packed_rows, outputs), jnp.float32),
        ),
        name="local_work",
    )

    terms = (kept + swap_cores(sent).astype(jnp.float32)).astype(jnp.bfloat16)
    shard = terms.shape[0] // plane
    terms = exchange(terms.reshape(plane, shard, outputs), PLANE)
    fgrad, terms = lax.optimization_barrier((fgrad, terms))
    fgrad = exchange(fgrad.reshape(PEERS, SLOTS, HELD, channels), LON)
    terms = jnp.sum(terms.astype(jnp.float32), axis=0)
    terms = sum_ring(terms.astype(jnp.bfloat16), 4)
    terms = sum_ring(terms, 1)
    total = (terms / images).astype(jnp.bfloat16)
    fgrad, total = lax.optimization_barrier((fgrad, total))
    total = gather_copies(total, PLANE)
    feature_grad = on_chip(
        unpack_body,
        jax.ShapeDtypeStruct((columns, rows, channels), act),
        (who, home),
        (fgrad.reshape(PEERS * SLOTS, HELD, channels),),
        name="unpack",
    )[None]
    feature_grad, total = lax.optimization_barrier((feature_grad, total))
    other = swap_cores(total)
    total = jnp.stack([jnp.where(core == 0, total, other), jnp.where(core == 0, other, total)])

    main = channels // plane
    point_grad = total[:, :, :main].reshape(point_w.shape)
    small = total[:, :, main:].reshape(branches, -1, outputs)
    per_tap = -(-channels // outputs)
    depth_grad = small[:, : 9 * per_tap].reshape(branches, 9, -1)[:, :, :channels].reshape(depth_w.shape)
    bias_grad = small[:, 9 * per_tap].astype(jnp.float32)
    return (feature_grad, depth_grad, point_grad, bias_grad)


def solution(mesh):
    fine = Mesh(mesh.devices.reshape(4, 4, 2, 2, 4, 2), DP + LON)
    placed = (P(DP, LON, None, None), P(), P(), P(), P(DP, LON, None, None))
    return jax.shard_map(
        per_device,
        mesh=fine,
        in_specs=placed,
        out_specs=(P(DP, LON, None, None), P(), P(), P()),
        check_vma=False,
    )
```

```python
import jax
import jax.numpy as jnp
import numpy as np
from jax import lax
from jax.experimental import pallas as pl
from jax.experimental.pallas import tpu as pltpu
from jax.sharding import Mesh
from jax.sharding import PartitionSpec as P

CLASS = 12
PAIRS = 6
PEERS = 8
SLOTS = 7
HELD = 8
LANES = 128

DP = ("zh", "zl", "xl", "core")
LON = ("y", "xh")
Z = ("zh", "zl")
PLANE = ("xl", "y", "xh")


def swap_cores(block):
    return lax.ppermute(block, "core", [(0, 1), (1, 0)])


def exchange(blocks, axes):
    return lax.all_to_all(blocks, axes, 0, 0, tiled=True)


def gather_copies(block, axes):
    peers = lax.axis_size(axes)
    return exchange(jnp.broadcast_to(block[None], (peers,) + block.shape), axes)


def sum_ring(own, apart):
    planes = lax.axis_size(Z)

    def fetch(block, ahead):
        return lax.ppermute(block, Z, [((i + ahead) % planes, i) for i in range(planes)])

    after = fetch(own, apart)
    before = fetch(own, -apart)
    far = fetch(after, apart)
    own, after, before, far = [x.astype(jnp.float32) for x in (own, after, before, far)]
    return (own + far) + (before + after)


def sum_pair(own, apart):
    planes = lax.axis_size("zl")
    return own + lax.ppermute(own, "zl", [(i, i ^ apart) for i in range(planes)])


def deal_units(columns):
    blocks = CLASS // 3
    owned = [[] for _ in range(PEERS)]
    for m in range(blocks):
        units = iter([(c, q) for q in range(PAIRS) for c in range(3 * m, 3 * m + 3)])
        for e in range(PEERS):
            owned[e] += [next(units) for _ in range(2 + (e % blocks == m))]
    home = np.zeros((PEERS, columns * PAIRS), np.int32)
    away = np.zeros((PEERS, columns * PAIRS), np.int32)
    used = np.zeros((PEERS, PEERS), np.int32)
    for e in range(PEERS):
        for u, (c, q) in enumerate(owned[e]):
            for k in range(6):
                d, j = divmod(c + CLASS * k, columns)
                home[d, j * PAIRS + q] = e * SLOTS + used[d, e]
                away[e, u * 6 + k] = d * SLOTS + used[d, e]
                used[d, e] += 1
    assert used.max() == SLOTS and used.min() == SLOTS - 1
    return home.reshape(-1), away.reshape(-1)


def blank_slots(ref, lon):
    for block in (3 - lon % 4, 7 - lon % 4):
        ref[block * SLOTS + SLOTS - 1] = jnp.zeros(ref.shape[1:], ref.dtype)


def pack_body(who_ref, home_hbm, feat_hbm, cot_hbm, out_ref, home_ref, feat_ref, cot_ref, table_sem, sems):
    columns, _, channels = feat_ref.shape
    lon = who_ref[0]
    table = pltpu.make_async_copy(home_hbm, home_ref, table_sem)
    table.start()

    def fetch(j):
        return [
            pltpu.make_async_copy(source.at[j], held.at[j], sems.at[n, j])
            for n, (source, held) in enumerate(((feat_hbm, feat_ref), (cot_hbm, cot_ref)))
        ]

    for j in range(columns):
        for copy in fetch(j):
            copy.start()
    blank_slots(out_ref, lon)
    table.wait()

    def column(j, carry):
        for copy in fetch(j):
            copy.wait()
        for source, start in ((feat_ref, 0), (cot_ref, channels)):
            width = source.shape[2]
            rows = source[j].astype(jnp.float32)
            for q in range(PAIRS):
                slot = home_ref[(lon * columns + j) * PAIRS + q]
                tile = jnp.concatenate([rows[12 * n + 2 * q : 12 * n + 2 * q + 2] for n in range(4)], axis=0)
                out_ref[slot, :, start : start + width] = tile.astype(out_ref.dtype)
        return carry

    lax.fori_loop(0, columns, column, 0)


def unpack_body(who_ref, home_ref, tiles_ref, out_ref):
    columns = out_ref.shape[0]
    lon = who_ref[0]

    def column(j, carry):
        tiles = [tiles_ref[home_ref[(lon * columns + j) * PAIRS + q]].astype(jnp.float32) for q in range(PAIRS)]
        rows = [tiles[q][2 * n : 2 * n + 2] for n in range(4) for q in range(PAIRS)]
        out_ref[j] = jnp.concatenate(rows, axis=0).astype(out_ref.dtype)
        return carry

    lax.fori_loop(0, columns, column, 0)


def on_chip(body, out_shape, scalars, arrays, scratch=(), name=None, space=pltpu.VMEM):
    vmem = pl.BlockSpec(memory_space=pltpu.VMEM)
    smem = pl.BlockSpec(memory_space=pltpu.SMEM)
    return pl.pallas_call(
        body,
        out_shape=out_shape,
        in_specs=[smem] * len(scalars) + [pl.BlockSpec(memory_space=space)] * len(arrays),
        out_specs=jax.tree.map(lambda _: vmem, out_shape),
        scratch_shapes=list(scratch),
        compiler_params=pltpu.CompilerParams(vmem_limit_bytes=48 << 20),
        name=name,
    )(*scalars, *arrays)


def gate_slope(pre_act):
    sigmoid_val = jax.nn.sigmoid(pre_act)
    return sigmoid_val * (1.0 + pre_act * (1.0 - sigmoid_val))


def half_turn(tile):
    return pltpu.roll(tile, 4, 0)


def ends_swapped(tile, top):
    return jnp.where(top, pltpu.roll(tile, 2, 0), pltpu.roll(tile, 6, 0))


def shard_row(row, main, extra):
    return (row // extra) * (main + extra) + main + row % extra


def local_body(
    who_ref, core_ref, away_ref, cls_ref, taps_ref, pw_ref, pb_ref, kept_ref, sent_ref, fg_ref, depth, dgr, upstream, terms
):
    channels, outputs = pw_ref.shape[1:]
    shard = terms.shape[1] // 16
    main = channels // 16
    extra = shard - main
    tiles = channels // LANES
    wide = outputs // LANES
    per_tap = -(-tiles // wide)
    sub = lax.broadcasted_iota(jnp.int32, (HELD, LANES), 0)
    top = sub < 4
    first = sub < 2
    end = sub >= 6

    def tap(branch, a, e, lanes):
        row = branch * 9 + (a + 1) * 3 + e + 1
        return jnp.broadcast_to(taps_ref[row : row + 1, lanes], (HELD, LANES))

    def ends(up, down):
        return jnp.where(first, up, jnp.where(end, down, 0.0))

    def both(branch, a, lanes):
        return tap(branch, a, -1, lanes) + tap(branch, a, 1, lanes)

    units = depth.shape[1] // (6 * HELD)
    lon = who_ref[0]
    blank_slots(fg_ref, lon)

    def slots(u):
        return [away_ref[(lon * units + u) * 6 + k] for k in range(6)]

    def pair_rows(u, k):
        return pl.ds(pl.multiple_of((u * 6 + k) * HELD, 16), 16)

    def read_pairs(ref, branch, u, lanes):
        out = []
        for k in range(0, 6, 2):
            pair = ref[branch, pair_rows(u, k), lanes].astype(jnp.float32)
            out += [pair[:HELD], pair[HELD:]]
        return out

    def write_pairs(ref, branch, u, lanes, made):
        for k in range(0, 6, 2):
            pair = jnp.concatenate([made[k], made[k + 1]], axis=0)
            ref[branch, pair_rows(u, k), lanes] = pair.astype(jnp.bfloat16)

    def gather_upstream(u, carry):
        at = slots(u)
        for k in range(0, 6, 2):
            for c in range(channels, cls_ref.shape[2], LANES):
                lanes = slice(c, c + LANES)
                pair = jnp.concatenate([cls_ref[at[k + n], :, lanes].astype(jnp.float32) for n in range(2)], axis=0)
                upstream[pair_rows(u, k), c - channels : c - channels + LANES] = pair
        return carry

    lax.fori_loop(0, units, gather_upstream, 0)

    for t in range(tiles):
        lanes = slice(t * LANES, (t + 1) * LANES)
        mid_a = [tap(0, 0, e, lanes) for e in (-1, 0, 1)]
        off_a = [jnp.where(top, tap(0, 1, e, lanes), tap(0, -1, e, lanes)) for e in (-1, 0, 1)]
        mid_b = [tap(1, 0, 0, lanes), both(1, 0, lanes)]
        off_b = [
            ends(tap(1, 1, 0, lanes), tap(1, -1, 0, lanes)),
            ends(both(1, 1, lanes), both(1, -1, lanes)),
        ]

        def forward(u, carry):
            xs = [cls_ref[slot, :, lanes].astype(jnp.float32) for slot in slots(u)]
            turned = [half_turn(x) for x in xs]
            swapped = [ends_swapped(x, top) for x in xs]
            made_a = [
                sum(
                    mid_a[n] * xs[(k + 2 * n - 2) % 6] + off_a[n] * turned[(k + 2 * n - 2) % 6] for n in range(3)
                )
                for k in range(6)
            ]
            made_b = [
                mid_b[0] * xs[k]
                + mid_b[1] * xs[(k + 3) % 6]
                + off_b[0] * swapped[k]
                + off_b[1] * swapped[(k + 3) % 6]
                for k in range(6)
            ]
            write_pairs(depth, 0, u, lanes, made_a)
            write_pairs(depth, 1, u, lanes, made_b)
            return carry

        lax.fori_loop(0, units, forward, 0, unroll=True)

    for branch in range(2):
        act = jnp.dot(depth[branch], pw_ref[branch], preferred_element_type=jnp.float32)
        act = act + pb_ref[branch : branch + 1, :]
        up = upstream[:, branch * outputs : (branch + 1) * outputs]
        pgrad = (up * gate_slope(act)).astype(jnp.bfloat16)
        point = lax.dot_general(
            depth[branch], pgrad, (((0,), (0,)), ((), ())), preferred_element_type=jnp.float32
        )
        for p in range(16):
            terms[branch, p * shard : p * shard + main, :] = point[p * main : (p + 1) * main]
            terms[branch, p * shard + main : (p + 1) * shard, :] = jnp.zeros((extra, outputs), jnp.float32)
        row = shard_row(9 * per_tap, main, extra)
        terms[branch, row : row + 1, :] = jnp.sum(pgrad.astype(jnp.float32), axis=0, keepdims=True)
        for c in range(0, channels, 384):
            part = lax.dot_general(
                pgrad, pw_ref[branch, c : c + 384, :], (((1,), (1,)), ((), ())), preferred_element_type=jnp.float32
            )
            dgr[branch, :, c : c + 384] = part.astype(jnp.bfloat16)

    for t in range(tiles):
        lanes = slice(t * LANES, (t + 1) * LANES)
        mid_a = [tap(0, 0, e, lanes) for e in (-1, 0, 1)]
        off_a = [jnp.where(top, tap(0, -1, e, lanes), tap(0, 1, e, lanes)) for e in (-1, 0, 1)]
        mid_b = [tap(1, 0, 0, lanes), both(1, 0, lanes)]
        off_b = [
            ends(tap(1, -1, 0, lanes), tap(1, 1, 0, lanes)),
            ends(both(1, -1, lanes), both(1, 1, lanes)),
        ]

        def backward(u, sums):
            sums = list(sums)
            at = slots(u)
            xs = [cls_ref[slot, :, lanes].astype(jnp.float32) for slot in at]
            das = read_pairs(dgr, 0, u, lanes)
            dbs = read_pairs(dgr, 1, u, lanes)
            turned = [half_turn(d) for d in das]
            swapped = [ends_swapped(d, top) for d in dbs]
            for k in range(6):
                made = (
                    sum(
                        mid_a[n] * das[(k - 2 * n + 2) % 6] + off_a[n] * turned[(k - 2 * n + 2) % 6]
                        for n in range(3)
                    )
                    + mid_b[0] * dbs[k]
                    + mid_b[1] * dbs[(k + 3) % 6]
                    + off_b[0] * swapped[k]
                    + off_b[1] * swapped[(k + 3) % 6]
                )
                fg_ref[at[k], :, lanes] = made.astype(jnp.bfloat16)
            for n in range(3):
                sums[n] += sum(xs[(k + 2 * n - 2) % 6] * das[k] for k in range(6))
                sums[3 + n] += sum(xs[(k + 2 * n - 2) % 6] * turned[k] for k in range(6))
            for n in range(2):
                sums[6 + n] += sum(xs[(k + 3 * n) % 6] * dbs[k] for k in range(6))
                sums[8 + n] += sum(xs[(k + 3 * n) % 6] * swapped[k] for k in range(6))
            return tuple(sums)

        zero = jnp.zeros((HELD, LANES), jnp.float32)
        sums = lax.fori_loop(0, units, backward, (zero,) * 10, unroll=True)

        def keep(branch, a, e, value, mask=None):
            value = value if mask is None else jnp.where(mask, value, 0.0)
            row = shard_row(((a + 1) * 3 + e + 1) * per_tap + t // wide, main, extra)
            at = (t % wide) * LANES
            terms[branch, row : row + 1, at : at + LANES] = jnp.sum(value, axis=0, keepdims=True)

        for n in range(3):
            keep(0, 0, n - 1, sums[n])
            keep(0, 1, n - 1, sums[3 + n], jnp.logical_not(top))
            keep(0, -1, n - 1, sums[3 + n], top)
        for e in (-1, 0, 1):
            keep(1, 0, e, sums[6 + abs(e)])
            keep(1, 1, e, sums[8 + abs(e)], end)
            keep(1, -1, e, sums[8 + abs(e)], first)

    @pl.when(core_ref[0] == 0)
    def _():
        kept_ref[...] = terms[0]
        sent_ref[...] = terms[1].astype(jnp.bfloat16)

    @pl.when(core_ref[0] != 0)
    def _():
        kept_ref[...] = terms[1]
        sent_ref[...] = terms[0].astype(jnp.bfloat16)


def per_device(features, depth_w, point_w, point_bias, cotangent):
    _, columns, rows, channels = features.shape
    branches, _, outputs = point_w.shape
    images = lax.axis_size(DP) * features.shape[0]
    plane = lax.axis_size(PLANE)
    core = lax.axis_index("core")
    who = lax.axis_index(LON).reshape(1)
    home, away = deal_units(columns)
    cells = columns * rows
    packed_rows = 16 * (channels // 16 + 8)
    width = channels + cotangent.shape[3]
    act = jnp.bfloat16

    packed = on_chip(
        pack_body,
        jax.ShapeDtypeStruct((PEERS * SLOTS, HELD, width), act),
        (who,),
        [pltpu.with_memory_space_constraint(x, pltpu.HBM) for x in (home, features[0], cotangent[0])],
        (
            pltpu.SMEM(home.shape, jnp.int32),
            pltpu.VMEM((columns, rows, channels), act),
            pltpu.VMEM((columns, rows, cotangent.shape[3]), act),
            pltpu.SemaphoreType.DMA(()),
            pltpu.SemaphoreType.DMA((2, columns)),
        ),
        name="pack",
        space=pltpu.HBM,
    )
    field = exchange(packed.reshape(PEERS, SLOTS, HELD, width), LON).reshape(packed.shape)
    taps = depth_w.astype(jnp.float32).reshape(branches * 9, channels)
    kept, sent, fgrad = on_chip(
        local_body,
        (
            jax.ShapeDtypeStruct((packed_rows, outputs), jnp.float32),
            jax.ShapeDtypeStruct((packed_rows, outputs), act),
            jax.ShapeDtypeStruct((PEERS * SLOTS, HELD, channels), act),
        ),
        (who, core.reshape(1), away),
        (field, taps, point_w, point_bias),
        (
            pltpu.VMEM((branches, cells, channels), act),
            pltpu.VMEM((branches, cells, channels), act),
            pltpu.VMEM((cells, branches * outputs), jnp.float32),
            pltpu.VMEM((branches, packed_rows, outputs), jnp.float32),
        ),
        name="local_work",
    )

    terms = (kept + swap_cores(sent).astype(jnp.float32)).astype(jnp.bfloat16)
    shard = terms.shape[0] // plane
    terms = exchange(terms.reshape(plane, shard, outputs), PLANE)
    fgrad, terms = lax.optimization_barrier((fgrad, terms))
    fgrad = exchange(fgrad.reshape(PEERS, SLOTS, HELD, channels), LON)
    terms = jnp.sum(terms.astype(jnp.float32), axis=0)
    terms = sum_pair(sum_pair(terms, 1), 2)
    terms = sum_ring(terms.astype(jnp.bfloat16), lax.axis_size("zl"))
    fgrad, terms = lax.optimization_barrier((fgrad, terms))
    total = (terms / images).astype(jnp.bfloat16)
    total = gather_copies(total, PLANE)
    feature_grad = on_chip(
        unpack_body,
        jax.ShapeDtypeStruct((columns, rows, channels), act),
        (who, home),
        (fgrad.reshape(PEERS * SLOTS, HELD, channels),),
        name="unpack",
    )[None]
    feature_grad, total = lax.optimization_barrier((feature_grad, total))
    other = swap_cores(total)
    total = jnp.stack([jnp.where(core == 0, total, other), jnp.where(core == 0, other, total)])

    main = channels // plane
    point_grad = total[:, :, :main].reshape(point_w.shape)
    small = total[:, :, main:].reshape(branches, -1, outputs)
    per_tap = -(-channels // outputs)
    depth_grad = small[:, : 9 * per_tap].reshape(branches, 9, -1)[:, :, :channels].reshape(depth_w.shape)
    bias_grad = small[:, 9 * per_tap].astype(jnp.float32)
    return (feature_grad, depth_grad, point_grad, bias_grad)


def solution(mesh):
    fine = Mesh(mesh.devices.reshape(4, 4, 2, 2, 4, 2), DP + LON)
    placed = (P(DP, LON, None, None), P(), P(), P(), P(DP, LON, None, None))
    return jax.shard_map(
        per_device,
        mesh=fine,
        in_specs=placed,
        out_specs=(P(DP, LON, None, None), P(), P(), P()),
        check_vma=False,
    )
```

```python
import jax
import jax.numpy as jnp
import numpy as np
from jax import lax
from jax.experimental import pallas as pl
from jax.experimental.pallas import tpu as pltpu
from jax.sharding import Mesh
from jax.sharding import PartitionSpec as P

CLASS = 12
PAIRS = 6
PEERS = 8
SLOTS = 7
HELD = 8
LANES = 128

DP = ("zh", "zl", "xl", "core")
LON = ("y", "xh")
Z = ("zh", "zl")
PLANE = ("xl", "y", "xh")


def swap_cores(block):
    return lax.ppermute(block, "core", [(0, 1), (1, 0)])


def exchange(blocks, axes):
    return lax.all_to_all(blocks, axes, 0, 0, tiled=True)


def gather_copies(block, axes):
    peers = lax.axis_size(axes)
    return exchange(jnp.broadcast_to(block[None], (peers,) + block.shape), axes)


def sum_ring(own, apart):
    planes = lax.axis_size(Z)

    def fetch(block, ahead):
        return lax.ppermute(block, Z, [((i + ahead) % planes, i) for i in range(planes)])

    after = fetch(own, apart)
    before = fetch(own, -apart)
    far = fetch(after, apart)
    own, after, before, far = [x.astype(jnp.float32) for x in (own, after, before, far)]
    return (own + far) + (before + after)


def sum_pair(own, apart):
    planes = lax.axis_size("zl")
    own = own.astype(jnp.bfloat16)
    other = lax.ppermute(own, "zl", [(i, i ^ apart) for i in range(planes)])
    return own.astype(jnp.float32) + other.astype(jnp.float32)


def deal_units(columns):
    blocks = CLASS // 3
    owned = [[] for _ in range(PEERS)]
    for m in range(blocks):
        units = iter([(c, q) for q in range(PAIRS) for c in range(3 * m, 3 * m + 3)])
        for e in range(PEERS):
            owned[e] += [next(units) for _ in range(2 + (e % blocks == m))]
    home = np.zeros((PEERS, columns * PAIRS), np.int32)
    away = np.zeros((PEERS, columns * PAIRS), np.int32)
    used = np.zeros((PEERS, PEERS), np.int32)
    for e in range(PEERS):
        for u, (c, q) in enumerate(owned[e]):
            for k in range(6):
                d, j = divmod(c + CLASS * k, columns)
                home[d, j * PAIRS + q] = e * SLOTS + used[d, e]
                away[e, u * 6 + k] = d * SLOTS + used[d, e]
                used[d, e] += 1
    assert used.max() == SLOTS and used.min() == SLOTS - 1
    return home.reshape(-1), away.reshape(-1)


def blank_slots(ref, lon):
    for block in (3 - lon % 4, 7 - lon % 4):
        ref[block * SLOTS + SLOTS - 1] = jnp.zeros(ref.shape[1:], ref.dtype)


def pack_body(who_ref, home_hbm, feat_hbm, cot_hbm, out_ref, home_ref, feat_ref, cot_ref, table_sem, sems):
    columns, _, channels = feat_ref.shape
    lon = who_ref[0]
    table = pltpu.make_async_copy(home_hbm, home_ref, table_sem)
    table.start()

    def fetch(j):
        return [
            pltpu.make_async_copy(source.at[j], held.at[j], sems.at[n, j])
            for n, (source, held) in enumerate(((feat_hbm, feat_ref), (cot_hbm, cot_ref)))
        ]

    for j in range(columns):
        for copy in fetch(j):
            copy.start()
    blank_slots(out_ref, lon)
    table.wait()

    def column(j, carry):
        for copy in fetch(j):
            copy.wait()
        for source, start in ((feat_ref, 0), (cot_ref, channels)):
            width = source.shape[2]
            rows = source[j].astype(jnp.float32)
            for q in range(PAIRS):
                slot = home_ref[(lon * columns + j) * PAIRS + q]
                tile = jnp.concatenate([rows[12 * n + 2 * q : 12 * n + 2 * q + 2] for n in range(4)], axis=0)
                out_ref[slot, :, start : start + width] = tile.astype(out_ref.dtype)
        return carry

    lax.fori_loop(0, columns, column, 0)


def unpack_body(who_ref, home_ref, tiles_ref, out_ref):
    columns = out_ref.shape[0]
    lon = who_ref[0]

    def column(j, carry):
        tiles = [tiles_ref[home_ref[(lon * columns + j) * PAIRS + q]].astype(jnp.float32) for q in range(PAIRS)]
        rows = [tiles[q][2 * n : 2 * n + 2] for n in range(4) for q in range(PAIRS)]
        out_ref[j] = jnp.concatenate(rows, axis=0).astype(out_ref.dtype)
        return carry

    lax.fori_loop(0, columns, column, 0)


def finish_body(core_ref, mine_ref, other_ref, point_ref, taps_ref, bias_ref):
    shards, held, outputs = mine_ref.shape
    channels = point_ref.shape[1]
    main = channels // shards
    per_tap = -(-channels // outputs)

    def branch_out(branch, source):
        for p in range(shards):
            point_ref[branch, p * main : (p + 1) * main, :] = source[p, :main]

        def extra(row):
            return source[row // (held - main), main + row % (held - main)].astype(jnp.float32)

        for n in range(9):
            for c in range(per_tap):
                width = min(outputs, channels - c * outputs)
                row = extra(n * per_tap + c)[:width]
                taps_ref[branch * 9 + n, c * outputs : c * outputs + width] = row.astype(taps_ref.dtype)
        bias_ref[branch] = extra(9 * per_tap)

    for first in (0, 1):

        @pl.when(core_ref[0] == first)
        def _():
            branch_out(first, mine_ref)
            branch_out(1 - first, other_ref)


def on_chip(body, out_shape, scalars, arrays, scratch=(), name=None, space=pltpu.VMEM):
    vmem = pl.BlockSpec(memory_space=pltpu.VMEM)
    smem = pl.BlockSpec(memory_space=pltpu.SMEM)
    return pl.pallas_call(
        body,
        out_shape=out_shape,
        in_specs=[smem] * len(scalars) + [pl.BlockSpec(memory_space=space)] * len(arrays),
        out_specs=jax.tree.map(lambda _: vmem, out_shape),
        scratch_shapes=list(scratch),
        compiler_params=pltpu.CompilerParams(vmem_limit_bytes=48 << 20),
        name=name,
    )(*scalars, *arrays)


def gate_slope(pre_act):
    sigmoid_val = jax.nn.sigmoid(pre_act)
    return sigmoid_val * (1.0 + pre_act * (1.0 - sigmoid_val))


def half_turn(tile):
    return pltpu.roll(tile, 4, 0)


def ends_swapped(tile, top):
    return jnp.where(top, pltpu.roll(tile, 2, 0), pltpu.roll(tile, 6, 0))


def shard_row(row, main, extra):
    return (row // extra) * (main + extra) + main + row % extra


def local_body(
    who_ref, core_ref, away_ref, cls_ref, taps_ref, pw_ref, pb_ref, kept_ref, sent_ref, fg_ref, depth, dgr, upstream, terms
):
    channels, outputs = pw_ref.shape[1:]
    shard = terms.shape[1] // 16
    main = channels // 16
    extra = shard - main
    tiles = channels // LANES
    wide = outputs // LANES
    per_tap = -(-tiles // wide)
    sub = lax.broadcasted_iota(jnp.int32, (HELD, LANES), 0)
    top = sub < 4
    first = sub < 2
    end = sub >= 6

    def tap(branch, a, e, lanes):
        row = branch * 9 + (a + 1) * 3 + e + 1
        return jnp.broadcast_to(taps_ref[row : row + 1, lanes], (HELD, LANES))

    def ends(up, down):
        return jnp.where(first, up, jnp.where(end, down, 0.0))

    def both(branch, a, lanes):
        return tap(branch, a, -1, lanes) + tap(branch, a, 1, lanes)

    units = depth.shape[1] // (6 * HELD)
    lon = who_ref[0]
    blank_slots(fg_ref, lon)

    def slots(u):
        return [away_ref[(lon * units + u) * 6 + k] for k in range(6)]

    def pair_rows(u, k):
        return pl.ds(pl.multiple_of((u * 6 + k) * HELD, 16), 16)

    def read_pairs(ref, branch, u, lanes):
        out = []
        for k in range(0, 6, 2):
            pair = ref[branch, pair_rows(u, k), lanes].astype(jnp.float32)
            out += [pair[:HELD], pair[HELD:]]
        return out

    def write_pairs(ref, branch, u, lanes, made):
        for k in range(0, 6, 2):
            pair = jnp.concatenate([made[k], made[k + 1]], axis=0)
            ref[branch, pair_rows(u, k), lanes] = pair.astype(jnp.bfloat16)

    def gather_upstream(u, carry):
        at = slots(u)
        for k in range(0, 6, 2):
            for c in range(channels, cls_ref.shape[2], LANES):
                lanes = slice(c, c + LANES)
                pair = jnp.concatenate([cls_ref[at[k + n], :, lanes].astype(jnp.float32) for n in range(2)], axis=0)
                upstream[pair_rows(u, k), c - channels : c - channels + LANES] = pair
        return carry

    lax.fori_loop(0, units, gather_upstream, 0)

    for t in range(tiles):
        lanes = slice(t * LANES, (t + 1) * LANES)
        mid_a = [tap(0, 0, e, lanes) for e in (-1, 0, 1)]
        off_a = [jnp.where(top, tap(0, 1, e, lanes), tap(0, -1, e, lanes)) for e in (-1, 0, 1)]
        mid_b = [tap(1, 0, 0, lanes), both(1, 0, lanes)]
        off_b = [
            ends(tap(1, 1, 0, lanes), tap(1, -1, 0, lanes)),
            ends(both(1, 1, lanes), both(1, -1, lanes)),
        ]

        def forward(u, carry):
            xs = [cls_ref[slot, :, lanes].astype(jnp.float32) for slot in slots(u)]
            turned = [half_turn(x) for x in xs]
            swapped = [ends_swapped(x, top) for x in xs]
            made_a = [
                sum(
                    mid_a[n] * xs[(k + 2 * n - 2) % 6] + off_a[n] * turned[(k + 2 * n - 2) % 6] for n in range(3)
                )
                for k in range(6)
            ]
            made_b = [
                mid_b[0] * xs[k]
                + mid_b[1] * xs[(k + 3) % 6]
                + off_b[0] * swapped[k]
                + off_b[1] * swapped[(k + 3) % 6]
                for k in range(6)
            ]
            write_pairs(depth, 0, u, lanes, made_a)
            write_pairs(depth, 1, u, lanes, made_b)
            return carry

        lax.fori_loop(0, units, forward, 0, unroll=True)

    for branch in range(2):
        act = jnp.dot(depth[branch], pw_ref[branch], preferred_element_type=jnp.float32)
        act = act + pb_ref[branch : branch + 1, :]
        up = upstream[:, branch * outputs : (branch + 1) * outputs]
        pgrad = (up * gate_slope(act)).astype(jnp.bfloat16)
        point = lax.dot_general(
            depth[branch], pgrad, (((0,), (0,)), ((), ())), preferred_element_type=jnp.float32
        )
        for p in range(16):
            terms[branch, p * shard : p * shard + main, :] = point[p * main : (p + 1) * main]
            terms[branch, p * shard + main : (p + 1) * shard, :] = jnp.zeros((extra, outputs), jnp.float32)
        row = shard_row(9 * per_tap, main, extra)
        terms[branch, row : row + 1, :] = jnp.sum(pgrad.astype(jnp.float32), axis=0, keepdims=True)
        for c in range(0, channels, 384):
            part = lax.dot_general(
                pgrad, pw_ref[branch, c : c + 384, :], (((1,), (1,)), ((), ())), preferred_element_type=jnp.float32
            )
            dgr[branch, :, c : c + 384] = part.astype(jnp.bfloat16)

    for t in range(tiles):
        lanes = slice(t * LANES, (t + 1) * LANES)
        mid_a = [tap(0, 0, e, lanes) for e in (-1, 0, 1)]
        off_a = [jnp.where(top, tap(0, -1, e, lanes), tap(0, 1, e, lanes)) for e in (-1, 0, 1)]
        mid_b = [tap(1, 0, 0, lanes), both(1, 0, lanes)]
        off_b = [
            ends(tap(1, -1, 0, lanes), tap(1, 1, 0, lanes)),
            ends(both(1, -1, lanes), both(1, 1, lanes)),
        ]

        def backward(u, sums):
            sums = list(sums)
            at = slots(u)
            xs = [cls_ref[slot, :, lanes].astype(jnp.float32) for slot in at]
            das = read_pairs(dgr, 0, u, lanes)
            dbs = read_pairs(dgr, 1, u, lanes)
            turned = [half_turn(d) for d in das]
            swapped = [ends_swapped(d, top) for d in dbs]
            for k in range(6):
                made = (
                    sum(
                        mid_a[n] * das[(k - 2 * n + 2) % 6] + off_a[n] * turned[(k - 2 * n + 2) % 6]
                        for n in range(3)
                    )
                    + mid_b[0] * dbs[k]
                    + mid_b[1] * dbs[(k + 3) % 6]
                    + off_b[0] * swapped[k]
                    + off_b[1] * swapped[(k + 3) % 6]
                )
                fg_ref[at[k], :, lanes] = made.astype(jnp.bfloat16)
            for n in range(3):
                sums[n] += sum(xs[(k + 2 * n - 2) % 6] * das[k] for k in range(6))
                sums[3 + n] += sum(xs[(k + 2 * n - 2) % 6] * turned[k] for k in range(6))
            for n in range(2):
                sums[6 + n] += sum(xs[(k + 3 * n) % 6] * dbs[k] for k in range(6))
                sums[8 + n] += sum(xs[(k + 3 * n) % 6] * swapped[k] for k in range(6))
            return tuple(sums)

        zero = jnp.zeros((HELD, LANES), jnp.float32)
        sums = lax.fori_loop(0, units, backward, (zero,) * 10, unroll=True)

        def keep(branch, a, e, value, mask=None):
            value = value if mask is None else jnp.where(mask, value, 0.0)
            row = shard_row(((a + 1) * 3 + e + 1) * per_tap + t // wide, main, extra)
            at = (t % wide) * LANES
            terms[branch, row : row + 1, at : at + LANES] = jnp.sum(value, axis=0, keepdims=True)

        for n in range(3):
            keep(0, 0, n - 1, sums[n])
            keep(0, 1, n - 1, sums[3 + n], jnp.logical_not(top))
            keep(0, -1, n - 1, sums[3 + n], top)
        for e in (-1, 0, 1):
            keep(1, 0, e, sums[6 + abs(e)])
            keep(1, 1, e, sums[8 + abs(e)], end)
            keep(1, -1, e, sums[8 + abs(e)], first)

    @pl.when(core_ref[0] == 0)
    def _():
        kept_ref[...] = terms[0]
        sent_ref[...] = terms[1].astype(jnp.bfloat16)

    @pl.when(core_ref[0] != 0)
    def _():
        kept_ref[...] = terms[1]
        sent_ref[...] = terms[0].astype(jnp.bfloat16)


def per_device(features, depth_w, point_w, point_bias, cotangent):
    _, columns, rows, channels = features.shape
    branches, _, outputs = point_w.shape
    images = lax.axis_size(DP) * features.shape[0]
    plane = lax.axis_size(PLANE)
    core = lax.axis_index("core")
    who = lax.axis_index(LON).reshape(1)
    home, away = deal_units(columns)
    cells = columns * rows
    packed_rows = 16 * (channels // 16 + 8)
    width = channels + cotangent.shape[3]
    act = jnp.bfloat16

    packed = on_chip(
        pack_body,
        jax.ShapeDtypeStruct((PEERS * SLOTS, HELD, width), act),
        (who,),
        [pltpu.with_memory_space_constraint(x, pltpu.HBM) for x in (home, features[0], cotangent[0])],
        (
            pltpu.SMEM(home.shape, jnp.int32),
            pltpu.VMEM((columns, rows, channels), act),
            pltpu.VMEM((columns, rows, cotangent.shape[3]), act),
            pltpu.SemaphoreType.DMA(()),
            pltpu.SemaphoreType.DMA((2, columns)),
        ),
        name="pack",
        space=pltpu.HBM,
    )
    field = exchange(packed.reshape(PEERS, SLOTS, HELD, width), LON).reshape(packed.shape)
    taps = depth_w.astype(jnp.float32).reshape(branches * 9, channels)
    kept, sent, fgrad = on_chip(
        local_body,
        (
            jax.ShapeDtypeStruct((packed_rows, outputs), jnp.float32),
            jax.ShapeDtypeStruct((packed_rows, outputs), act),
            jax.ShapeDtypeStruct((PEERS * SLOTS, HELD, channels), act),
        ),
        (who, core.reshape(1), away),
        (field, taps, point_w, point_bias),
        (
            pltpu.VMEM((branches, cells, channels), act),
            pltpu.VMEM((branches, cells, channels), act),
            pltpu.VMEM((cells, branches * outputs), jnp.float32),
            pltpu.VMEM((branches, packed_rows, outputs), jnp.float32),
        ),
        name="local_work",
    )

    terms = (kept + swap_cores(sent).astype(jnp.float32)).astype(jnp.bfloat16)
    shard = terms.shape[0] // plane
    terms = exchange(terms.reshape(plane, shard, outputs), PLANE)
    terms = jnp.sum(terms.astype(jnp.float32), axis=0)
    fgrad, terms = lax.optimization_barrier((fgrad, terms))
    fgrad = exchange(fgrad.reshape(PEERS, SLOTS, HELD, channels), LON)
    terms = sum_pair(sum_pair(terms, 1), 2)
    terms = sum_ring(terms.astype(jnp.bfloat16), lax.axis_size("zl"))
    fgrad, terms = lax.optimization_barrier((fgrad, terms))
    total = (terms / images).astype(jnp.bfloat16)
    total = gather_copies(total, PLANE)
    feature_grad = on_chip(
        unpack_body,
        jax.ShapeDtypeStruct((columns, rows, channels), act),
        (who, home),
        (fgrad.reshape(PEERS * SLOTS, HELD, channels),),
        name="unpack",
    )[None]
    feature_grad, total = lax.optimization_barrier((feature_grad, total))
    other = swap_cores(total)
    point_grad, depth_grad, bias_grad = on_chip(
        finish_body,
        (
            jax.ShapeDtypeStruct(point_w.shape, act),
            jax.ShapeDtypeStruct((branches * 9, channels), act),
            jax.ShapeDtypeStruct(point_bias.shape, jnp.float32),
        ),
        (core.reshape(1),),
        (total, other),
        name="finish",
    )
    depth_grad = depth_grad.reshape(depth_w.shape)
    return (feature_grad, depth_grad, point_grad, bias_grad)


def solution(mesh):
    fine = Mesh(mesh.devices.reshape(4, 4, 2, 2, 4, 2), DP + LON)
    placed = (P(DP, LON, None, None), P(), P(), P(), P(DP, LON, None, None))
    return jax.shard_map(
        per_device,
        mesh=fine,
        in_specs=placed,
        out_specs=(P(DP, LON, None, None), P(), P(), P()),
        check_vma=False,
    )
```

```python
import jax
import jax.numpy as jnp
import numpy as np
from jax import lax
from jax.experimental import pallas as pl
from jax.experimental.pallas import tpu as pltpu
from jax.sharding import Mesh
from jax.sharding import PartitionSpec as P

CLASS = 12
PAIRS = 6
PEERS = 8
SLOTS = 7
HELD = 8
LANES = 128

DP = ("zh", "zl", "xl", "core")
LON = ("y", "xh")
Z = ("zh", "zl")
PLANE = ("xl", "y", "xh")


def swap_cores(block):
    return lax.ppermute(block, "core", [(0, 1), (1, 0)])


def exchange(blocks, axes):
    return lax.all_to_all(blocks, axes, 0, 0, tiled=True)


def gather_copies(block, axes):
    peers = lax.axis_size(axes)
    return exchange(jnp.broadcast_to(block[None], (peers,) + block.shape), axes)


def sum_ring(own, apart):
    planes = lax.axis_size(Z)

    def fetch(block, ahead):
        return lax.ppermute(block, Z, [((i + ahead) % planes, i) for i in range(planes)])

    after = fetch(own, apart)
    before = fetch(own, -apart)
    far = fetch(after, apart)
    own, after, before, far = [x.astype(jnp.float32) for x in (own, after, before, far)]
    return (own + far) + (before + after)


def sum_pair(own, apart):
    planes = lax.axis_size("zl")
    own = own.astype(jnp.bfloat16)
    other = lax.ppermute(own, "zl", [(i, i ^ apart) for i in range(planes)])
    return own.astype(jnp.float32) + other.astype(jnp.float32)


def deal_units(columns):
    blocks = CLASS // 3
    owned = [[] for _ in range(PEERS)]
    for m in range(blocks):
        units = iter([(c, q) for q in range(PAIRS) for c in range(3 * m, 3 * m + 3)])
        for e in range(PEERS):
            owned[e] += [next(units) for _ in range(2 + (e % blocks == m))]
    home = np.zeros((PEERS, columns * PAIRS), np.int32)
    away = np.zeros((PEERS, columns * PAIRS), np.int32)
    used = np.zeros((PEERS, PEERS), np.int32)
    for e in range(PEERS):
        for u, (c, q) in enumerate(owned[e]):
            for k in range(6):
                d, j = divmod(c + CLASS * k, columns)
                home[d, j * PAIRS + q] = e * SLOTS + used[d, e]
                away[e, u * 6 + k] = d * SLOTS + used[d, e]
                used[d, e] += 1
    assert used.max() == SLOTS and used.min() == SLOTS - 1
    return home.reshape(-1), away.reshape(-1)


def blank_slots(ref, lon):
    for block in (3 - lon % 4, 7 - lon % 4):
        ref[block * SLOTS + SLOTS - 1] = jnp.zeros(ref.shape[1:], ref.dtype)


def pack_body(who_ref, home_hbm, feat_hbm, cot_hbm, out_ref, home_ref, feat_ref, cot_ref, table_sem, sems):
    columns, _, channels = feat_ref.shape
    lon = who_ref[0]
    table = pltpu.make_async_copy(home_hbm, home_ref, table_sem)
    table.start()

    def fetch(j):
        return [
            pltpu.make_async_copy(source.at[j], held.at[j], sems.at[n, j])
            for n, (source, held) in enumerate(((feat_hbm, feat_ref), (cot_hbm, cot_ref)))
        ]

    for j in range(columns):
        for copy in fetch(j):
            copy.start()
    blank_slots(out_ref, lon)
    table.wait()

    def column(j, carry):
        for copy in fetch(j):
            copy.wait()
        for source, start in ((feat_ref, 0), (cot_ref, channels)):
            width = source.shape[2]
            rows = source[j].astype(jnp.float32)
            for q in range(PAIRS):
                slot = home_ref[(lon * columns + j) * PAIRS + q]
                tile = jnp.concatenate([rows[12 * n + 2 * q : 12 * n + 2 * q + 2] for n in range(4)], axis=0)
                out_ref[slot, :, start : start + width] = tile.astype(out_ref.dtype)
        return carry

    lax.fori_loop(0, columns, column, 0)


def unpack_body(who_ref, home_ref, tiles_ref, out_ref):
    columns = out_ref.shape[0]
    lon = who_ref[0]

    def column(j, carry):
        tiles = [tiles_ref[home_ref[(lon * columns + j) * PAIRS + q]].astype(jnp.float32) for q in range(PAIRS)]
        rows = [tiles[q][2 * n : 2 * n + 2] for n in range(4) for q in range(PAIRS)]
        out_ref[j] = jnp.concatenate(rows, axis=0).astype(out_ref.dtype)
        return carry

    lax.fori_loop(0, columns, column, 0)


def finish_body(core_ref, mine_ref, other_ref, point_ref, taps_ref, bias_ref):
    shards, held, outputs = mine_ref.shape
    channels = point_ref.shape[1]
    main = channels // shards
    per_tap = -(-channels // outputs)

    def branch_out(branch, source):
        for p in range(shards):
            point_ref[branch, p * main : (p + 1) * main, :] = source[p, :main]

        def extra(row):
            return source[row // (held - main), main + row % (held - main)].astype(jnp.float32)

        for n in range(9):
            for c in range(per_tap):
                width = min(outputs, channels - c * outputs)
                row = extra(n * per_tap + c)[:width]
                taps_ref[n, branch, c * outputs : c * outputs + width] = row.astype(taps_ref.dtype)
        bias_ref[branch] = extra(9 * per_tap)

    for first in (0, 1):

        @pl.when(core_ref[0] == first)
        def _():
            branch_out(first, mine_ref)
            branch_out(1 - first, other_ref)


def on_chip(body, out_shape, scalars, arrays, scratch=(), name=None, space=pltpu.VMEM):
    vmem = pl.BlockSpec(memory_space=pltpu.VMEM)
    smem = pl.BlockSpec(memory_space=pltpu.SMEM)
    return pl.pallas_call(
        body,
        out_shape=out_shape,
        in_specs=[smem] * len(scalars) + [pl.BlockSpec(memory_space=space)] * len(arrays),
        out_specs=jax.tree.map(lambda _: vmem, out_shape),
        scratch_shapes=list(scratch),
        compiler_params=pltpu.CompilerParams(vmem_limit_bytes=48 << 20),
        name=name,
    )(*scalars, *arrays)


def gate_slope(pre_act):
    sigmoid_val = jax.nn.sigmoid(pre_act)
    return sigmoid_val * (1.0 + pre_act * (1.0 - sigmoid_val))


def half_turn(tile):
    return pltpu.roll(tile, 4, 0)


def ends_swapped(tile, top):
    return jnp.where(top, pltpu.roll(tile, 2, 0), pltpu.roll(tile, 6, 0))


def shard_row(row, main, extra):
    return (row // extra) * (main + extra) + main + row % extra


def local_body(
    who_ref, core_ref, away_ref, cls_ref, taps_ref, pw_ref, pb_ref, kept_ref, sent_ref, fg_ref, depth, dgr, upstream, terms
):
    channels, outputs = pw_ref.shape[1:]
    shard = terms.shape[1] // 16
    main = channels // 16
    extra = shard - main
    tiles = channels // LANES
    wide = outputs // LANES
    per_tap = -(-tiles // wide)
    sub = lax.broadcasted_iota(jnp.int32, (HELD, LANES), 0)
    top = sub < 4
    first = sub < 2
    end = sub >= 6

    def tap(branch, a, e, lanes):
        row = branch * 9 + (a + 1) * 3 + e + 1
        return jnp.broadcast_to(taps_ref[row : row + 1, lanes], (HELD, LANES))

    def ends(up, down):
        return jnp.where(first, up, jnp.where(end, down, 0.0))

    def both(branch, a, lanes):
        return tap(branch, a, -1, lanes) + tap(branch, a, 1, lanes)

    units = depth.shape[1] // (6 * HELD)
    lon = who_ref[0]
    blank_slots(fg_ref, lon)

    def slots(u):
        return [away_ref[(lon * units + u) * 6 + k] for k in range(6)]

    def pair_rows(u, k):
        return pl.ds(pl.multiple_of((u * 6 + k) * HELD, 16), 16)

    def read_pairs(ref, branch, u, lanes):
        out = []
        for k in range(0, 6, 2):
            pair = ref[branch, pair_rows(u, k), lanes].astype(jnp.float32)
            out += [pair[:HELD], pair[HELD:]]
        return out

    def write_pairs(ref, branch, u, lanes, made):
        for k in range(0, 6, 2):
            pair = jnp.concatenate([made[k], made[k + 1]], axis=0)
            ref[branch, pair_rows(u, k), lanes] = pair.astype(jnp.bfloat16)

    def gather_upstream(u, carry):
        at = slots(u)
        for k in range(0, 6, 2):
            for c in range(channels, cls_ref.shape[2], LANES):
                lanes = slice(c, c + LANES)
                pair = jnp.concatenate([cls_ref[at[k + n], :, lanes].astype(jnp.float32) for n in range(2)], axis=0)
                upstream[pair_rows(u, k), c - channels : c - channels + LANES] = pair
        return carry

    lax.fori_loop(0, units, gather_upstream, 0)

    for t in range(tiles):
        lanes = slice(t * LANES, (t + 1) * LANES)
        mid_a = [tap(0, 0, e, lanes) for e in (-1, 0, 1)]
        off_a = [jnp.where(top, tap(0, 1, e, lanes), tap(0, -1, e, lanes)) for e in (-1, 0, 1)]
        mid_b = [tap(1, 0, 0, lanes), both(1, 0, lanes)]
        off_b = [
            ends(tap(1, 1, 0, lanes), tap(1, -1, 0, lanes)),
            ends(both(1, 1, lanes), both(1, -1, lanes)),
        ]

        def forward(u, carry):
            xs = [cls_ref[slot, :, lanes].astype(jnp.float32) for slot in slots(u)]
            turned = [half_turn(x) for x in xs]
            swapped = [ends_swapped(x, top) for x in xs]
            made_a = [
                sum(
                    mid_a[n] * xs[(k + 2 * n - 2) % 6] + off_a[n] * turned[(k + 2 * n - 2) % 6] for n in range(3)
                )
                for k in range(6)
            ]
            made_b = [
                mid_b[0] * xs[k]
                + mid_b[1] * xs[(k + 3) % 6]
                + off_b[0] * swapped[k]
                + off_b[1] * swapped[(k + 3) % 6]
                for k in range(6)
            ]
            write_pairs(depth, 0, u, lanes, made_a)
            write_pairs(depth, 1, u, lanes, made_b)
            return carry

        lax.fori_loop(0, units, forward, 0, unroll=True)

    for branch in range(2):
        act = jnp.dot(depth[branch], pw_ref[branch], preferred_element_type=jnp.float32)
        act = act + pb_ref[branch : branch + 1, :]
        up = upstream[:, branch * outputs : (branch + 1) * outputs]
        pgrad = (up * gate_slope(act)).astype(jnp.bfloat16)
        point = lax.dot_general(
            depth[branch], pgrad, (((0,), (0,)), ((), ())), preferred_element_type=jnp.float32
        )
        for p in range(16):
            terms[branch, p * shard : p * shard + main, :] = point[p * main : (p + 1) * main]
            terms[branch, p * shard + main : (p + 1) * shard, :] = jnp.zeros((extra, outputs), jnp.float32)
        row = shard_row(9 * per_tap, main, extra)
        terms[branch, row : row + 1, :] = jnp.sum(pgrad.astype(jnp.float32), axis=0, keepdims=True)
        for c in range(0, channels, 384):
            part = lax.dot_general(
                pgrad, pw_ref[branch, c : c + 384, :], (((1,), (1,)), ((), ())), preferred_element_type=jnp.float32
            )
            dgr[branch, :, c : c + 384] = part.astype(jnp.bfloat16)

    for t in range(tiles):
        lanes = slice(t * LANES, (t + 1) * LANES)
        mid_a = [tap(0, 0, e, lanes) for e in (-1, 0, 1)]
        off_a = [jnp.where(top, tap(0, -1, e, lanes), tap(0, 1, e, lanes)) for e in (-1, 0, 1)]
        mid_b = [tap(1, 0, 0, lanes), both(1, 0, lanes)]
        off_b = [
            ends(tap(1, -1, 0, lanes), tap(1, 1, 0, lanes)),
            ends(both(1, -1, lanes), both(1, 1, lanes)),
        ]

        def backward(u, sums):
            sums = list(sums)
            at = slots(u)
            xs = [cls_ref[slot, :, lanes].astype(jnp.float32) for slot in at]
            das = read_pairs(dgr, 0, u, lanes)
            dbs = read_pairs(dgr, 1, u, lanes)
            turned = [half_turn(d) for d in das]
            swapped = [ends_swapped(d, top) for d in dbs]
            for k in range(6):
                made = (
                    sum(
                        mid_a[n] * das[(k - 2 * n + 2) % 6] + off_a[n] * turned[(k - 2 * n + 2) % 6]
                        for n in range(3)
                    )
                    + mid_b[0] * dbs[k]
                    + mid_b[1] * dbs[(k + 3) % 6]
                    + off_b[0] * swapped[k]
                    + off_b[1] * swapped[(k + 3) % 6]
                )
                fg_ref[at[k], :, lanes] = made.astype(jnp.bfloat16)
            for n in range(3):
                sums[n] += sum(xs[(k + 2 * n - 2) % 6] * das[k] for k in range(6))
                sums[3 + n] += sum(xs[(k + 2 * n - 2) % 6] * turned[k] for k in range(6))
            for n in range(2):
                sums[6 + n] += sum(xs[(k + 3 * n) % 6] * dbs[k] for k in range(6))
                sums[8 + n] += sum(xs[(k + 3 * n) % 6] * swapped[k] for k in range(6))
            return tuple(sums)

        zero = jnp.zeros((HELD, LANES), jnp.float32)
        sums = lax.fori_loop(0, units, backward, (zero,) * 10, unroll=True)

        def keep(branch, a, e, value, mask=None):
            value = value if mask is None else jnp.where(mask, value, 0.0)
            row = shard_row(((a + 1) * 3 + e + 1) * per_tap + t // wide, main, extra)
            at = (t % wide) * LANES
            terms[branch, row : row + 1, at : at + LANES] = jnp.sum(value, axis=0, keepdims=True)

        for n in range(3):
            keep(0, 0, n - 1, sums[n])
            keep(0, 1, n - 1, sums[3 + n], jnp.logical_not(top))
            keep(0, -1, n - 1, sums[3 + n], top)
        for e in (-1, 0, 1):
            keep(1, 0, e, sums[6 + abs(e)])
            keep(1, 1, e, sums[8 + abs(e)], end)
            keep(1, -1, e, sums[8 + abs(e)], first)

    @pl.when(core_ref[0] == 0)
    def _():
        kept_ref[...] = terms[0]
        sent_ref[...] = terms[1].astype(jnp.bfloat16)

    @pl.when(core_ref[0] != 0)
    def _():
        kept_ref[...] = terms[1]
        sent_ref[...] = terms[0].astype(jnp.bfloat16)


def per_device(features, depth_w, point_w, point_bias, cotangent):
    _, columns, rows, channels = features.shape
    branches, _, outputs = point_w.shape
    images = lax.axis_size(DP) * features.shape[0]
    plane = lax.axis_size(PLANE)
    core = lax.axis_index("core")
    who = lax.axis_index(LON).reshape(1)
    home, away = deal_units(columns)
    cells = columns * rows
    packed_rows = 16 * (channels // 16 + 8)
    width = channels + cotangent.shape[3]
    act = jnp.bfloat16

    packed = on_chip(
        pack_body,
        jax.ShapeDtypeStruct((PEERS * SLOTS, HELD, width), act),
        (who,),
        [pltpu.with_memory_space_constraint(x, pltpu.HBM) for x in (home, features[0], cotangent[0])],
        (
            pltpu.SMEM(home.shape, jnp.int32),
            pltpu.VMEM((columns, rows, channels), act),
            pltpu.VMEM((columns, rows, cotangent.shape[3]), act),
            pltpu.SemaphoreType.DMA(()),
            pltpu.SemaphoreType.DMA((2, columns)),
        ),
        name="pack",
        space=pltpu.HBM,
    )
    field = exchange(packed.reshape(PEERS, SLOTS, HELD, width), LON).reshape(packed.shape)
    taps = depth_w.astype(jnp.float32).reshape(branches * 9, channels)
    kept, sent, fgrad = on_chip(
        local_body,
        (
            jax.ShapeDtypeStruct((packed_rows, outputs), jnp.float32),
            jax.ShapeDtypeStruct((packed_rows, outputs), act),
            jax.ShapeDtypeStruct((PEERS * SLOTS, HELD, channels), act),
        ),
        (who, core.reshape(1), away),
        (field, taps, point_w, point_bias),
        (
            pltpu.VMEM((branches, cells, channels), act),
            pltpu.VMEM((branches, cells, channels), act),
            pltpu.VMEM((cells, branches * outputs), jnp.float32),
            pltpu.VMEM((branches, packed_rows, outputs), jnp.float32),
        ),
        name="local_work",
    )

    terms = (kept + swap_cores(sent).astype(jnp.float32)).astype(jnp.bfloat16)
    shard = terms.shape[0] // plane
    terms = exchange(terms.reshape(plane, shard, outputs), PLANE)
    fgrad, terms = lax.optimization_barrier((fgrad, terms))
    fgrad = exchange(fgrad.reshape(PEERS, SLOTS, HELD, channels), LON)
    terms = jnp.sum(terms.astype(jnp.float32), axis=0)
    terms = sum_pair(sum_pair(terms, 1), 2)
    terms = sum_ring(terms.astype(jnp.bfloat16), lax.axis_size("zl"))
    fgrad, terms = lax.optimization_barrier((fgrad, terms))
    total = (terms / images).astype(jnp.bfloat16)
    total = gather_copies(total, PLANE)
    feature_grad = on_chip(
        unpack_body,
        jax.ShapeDtypeStruct((columns, rows, channels), act),
        (who, home),
        (fgrad.reshape(PEERS * SLOTS, HELD, channels),),
        name="unpack",
    )[None]
    feature_grad, total = lax.optimization_barrier((feature_grad, total))
    other = swap_cores(total)
    point_grad, depth_grad, bias_grad = on_chip(
        finish_body,
        (
            jax.ShapeDtypeStruct(point_w.shape, act),
            jax.ShapeDtypeStruct((9, branches, channels), act),
            jax.ShapeDtypeStruct(point_bias.shape, jnp.float32),
        ),
        (core.reshape(1),),
        (total, other),
        name="finish",
    )
    depth_grad = depth_grad.reshape(3, 3, branches, channels).transpose(2, 0, 1, 3)
    return (feature_grad, depth_grad, point_grad, bias_grad)


def solution(mesh):
    fine = Mesh(mesh.devices.reshape(4, 4, 2, 2, 4, 2), DP + LON)
    placed = (P(DP, LON, None, None), P(), P(), P(), P(DP, LON, None, None))
    return jax.shard_map(
        per_device,
        mesh=fine,
        in_specs=placed,
        out_specs=(P(DP, LON, None, None), P(), P(), P()),
        check_vma=False,
    )
```

```python
import jax
import jax.numpy as jnp
import numpy as np
from jax import lax
from jax.experimental import pallas as pl
from jax.experimental.pallas import tpu as pltpu
from jax.sharding import Mesh
from jax.sharding import PartitionSpec as P

CLASS = 12
PAIRS = 6
PEERS = 8
SLOTS = 7
HELD = 8
LANES = 128

DP = ("zh", "zl", "xl", "core")
LON = ("y", "xh")
Z = ("zh", "zl")
PLANE = ("xl", "y", "xh")


def swap_cores(block):
    return lax.ppermute(block, "core", [(0, 1), (1, 0)])


def exchange(blocks, axes):
    return lax.all_to_all(blocks, axes, 0, 0, tiled=True)


def gather_copies(block, axes):
    peers = lax.axis_size(axes)
    return exchange(jnp.broadcast_to(block[None], (peers,) + block.shape), axes)


def sum_ring(own, apart):
    planes = lax.axis_size(Z)

    def fetch(block, ahead):
        return lax.ppermute(block, Z, [((i + ahead) % planes, i) for i in range(planes)])

    after = fetch(own, apart)
    before = fetch(own, -apart)
    far = fetch(after, apart)
    own, after, before, far = [x.astype(jnp.float32) for x in (own, after, before, far)]
    return (own + far) + (before + after)


def sum_pair(own, apart):
    planes = lax.axis_size("zl")
    own = own.astype(jnp.bfloat16)
    other = lax.ppermute(own, "zl", [(i, i ^ apart) for i in range(planes)])
    return own.astype(jnp.float32) + other.astype(jnp.float32)


def deal_units(columns):
    blocks = CLASS // 3
    owned = [[] for _ in range(PEERS)]
    for m in range(blocks):
        units = iter([(c, q) for q in range(PAIRS) for c in range(3 * m, 3 * m + 3)])
        for e in range(PEERS):
            owned[e] += [next(units) for _ in range(2 + (e % blocks == m))]
    home = np.zeros((PEERS, columns * PAIRS), np.int32)
    away = np.zeros((PEERS, columns * PAIRS), np.int32)
    used = np.zeros((PEERS, PEERS), np.int32)
    for e in range(PEERS):
        for u, (c, q) in enumerate(owned[e]):
            for k in range(6):
                d, j = divmod(c + CLASS * k, columns)
                home[d, j * PAIRS + q] = e * SLOTS + used[d, e]
                away[e, u * 6 + k] = d * SLOTS + used[d, e]
                used[d, e] += 1
    assert used.max() == SLOTS and used.min() == SLOTS - 1
    return home.reshape(-1), away.reshape(-1)


def blank_slots(ref, lon):
    for block in (3 - lon % 4, 7 - lon % 4):
        ref[block * SLOTS + SLOTS - 1] = jnp.zeros(ref.shape[1:], ref.dtype)


def pack_body(who_ref, home_hbm, feat_hbm, cot_hbm, out_ref, home_ref, feat_ref, cot_ref, table_sem, sems):
    columns, _, channels = feat_ref.shape
    lon = who_ref[0]
    table = pltpu.make_async_copy(home_hbm, home_ref, table_sem)
    table.start()

    def fetch(j):
        return [
            pltpu.make_async_copy(source.at[j], held.at[j], sems.at[n, j])
            for n, (source, held) in enumerate(((feat_hbm, feat_ref), (cot_hbm, cot_ref)))
        ]

    for j in range(columns):
        for copy in fetch(j):
            copy.start()
    blank_slots(out_ref, lon)
    table.wait()

    def column(j, carry):
        for copy in fetch(j):
            copy.wait()
        for source, start in ((feat_ref, 0), (cot_ref, channels)):
            width = source.shape[2]
            rows = source[j].astype(jnp.float32)
            for q in range(PAIRS):
                slot = home_ref[(lon * columns + j) * PAIRS + q]
                tile = jnp.concatenate([rows[12 * n + 2 * q : 12 * n + 2 * q + 2] for n in range(4)], axis=0)
                out_ref[slot, :, start : start + width] = tile.astype(out_ref.dtype)
        return carry

    lax.fori_loop(0, columns, column, 0)


def unpack_body(who_ref, home_ref, tiles_ref, out_ref):
    columns = out_ref.shape[0]
    lon = who_ref[0]

    def column(j, carry):
        tiles = [tiles_ref[home_ref[(lon * columns + j) * PAIRS + q]].astype(jnp.float32) for q in range(PAIRS)]
        rows = [tiles[q][2 * n : 2 * n + 2] for n in range(4) for q in range(PAIRS)]
        out_ref[j] = jnp.concatenate(rows, axis=0).astype(out_ref.dtype)
        return carry

    lax.fori_loop(0, columns, column, 0)


def finish_body(core_ref, mine_ref, other_ref, point_ref, taps_ref, bias_ref):
    shards, held, outputs = mine_ref.shape
    channels = point_ref.shape[1]
    main = channels // shards
    per_tap = -(-channels // outputs)

    def branch_out(branch, source):
        for p in range(shards):
            point_ref[branch, p * main : (p + 1) * main, :] = source[p, :main]

        def extra(row):
            return source[row // (held - main), main + row % (held - main)].astype(jnp.float32)

        for n in range(9):
            for c in range(per_tap):
                width = min(outputs, channels - c * outputs)
                row = extra(n * per_tap + c)[:width]
                taps_ref[n, branch, c * outputs : c * outputs + width] = row.astype(taps_ref.dtype)
        bias_ref[branch] = extra(9 * per_tap)

    for first in (0, 1):

        @pl.when(core_ref[0] == first)
        def _():
            branch_out(first, mine_ref)
            branch_out(1 - first, other_ref)


def on_chip(body, out_shape, scalars, arrays, scratch=(), name=None, space=pltpu.VMEM):
    vmem = pl.BlockSpec(memory_space=pltpu.VMEM)
    smem = pl.BlockSpec(memory_space=pltpu.SMEM)
    return pl.pallas_call(
        body,
        out_shape=out_shape,
        in_specs=[smem] * len(scalars) + [pl.BlockSpec(memory_space=space)] * len(arrays),
        out_specs=jax.tree.map(lambda _: vmem, out_shape),
        scratch_shapes=list(scratch),
        compiler_params=pltpu.CompilerParams(vmem_limit_bytes=48 << 20),
        name=name,
    )(*scalars, *arrays)


def gate_slope(pre_act):
    sigmoid_val = jax.nn.sigmoid(pre_act)
    return sigmoid_val * (1.0 + pre_act * (1.0 - sigmoid_val))


def half_turn(tile):
    return pltpu.roll(tile, 4, 0)


def ends_swapped(tile, top):
    return jnp.where(top, pltpu.roll(tile, 2, 0), pltpu.roll(tile, 6, 0))


def shard_row(row, main, extra):
    return (row // extra) * (main + extra) + main + row % extra


def local_body(
    who_ref, core_ref, away_ref, cls_ref, taps_ref, pw_ref, pb_ref, kept_ref, sent_ref, fg_ref, depth, dgr, upstream, terms
):
    channels, outputs = pw_ref.shape[1:]
    shard = terms.shape[1] // 16
    main = channels // 16
    extra = shard - main
    tiles = channels // LANES
    wide = outputs // LANES
    per_tap = -(-tiles // wide)
    sub = lax.broadcasted_iota(jnp.int32, (HELD, LANES), 0)
    top = sub < 4
    first = sub < 2
    end = sub >= 6

    def tap(branch, a, e, lanes):
        row = branch * 9 + (a + 1) * 3 + e + 1
        return jnp.broadcast_to(taps_ref[row : row + 1, lanes], (HELD, LANES))

    def ends(up, down):
        return jnp.where(first, up, jnp.where(end, down, 0.0))

    def both(branch, a, lanes):
        return tap(branch, a, -1, lanes) + tap(branch, a, 1, lanes)

    units = depth.shape[1] // (6 * HELD)
    lon = who_ref[0]
    blank_slots(fg_ref, lon)

    def slots(u):
        return [away_ref[(lon * units + u) * 6 + k] for k in range(6)]

    def pair_rows(u, k):
        return pl.ds(pl.multiple_of((u * 6 + k) * HELD, 16), 16)

    def read_pairs(ref, branch, u, lanes):
        out = []
        for k in range(0, 6, 2):
            pair = ref[branch, pair_rows(u, k), lanes].astype(jnp.float32)
            out += [pair[:HELD], pair[HELD:]]
        return out

    def write_pairs(ref, branch, u, lanes, made):
        for k in range(0, 6, 2):
            pair = jnp.concatenate([made[k], made[k + 1]], axis=0)
            ref[branch, pair_rows(u, k), lanes] = pair.astype(jnp.bfloat16)

    def gather_upstream(u, carry):
        at = slots(u)
        for k in range(0, 6, 2):
            for c in range(channels, cls_ref.shape[2], LANES):
                lanes = slice(c, c + LANES)
                pair = jnp.concatenate([cls_ref[at[k + n], :, lanes].astype(jnp.float32) for n in range(2)], axis=0)
                upstream[pair_rows(u, k), c - channels : c - channels + LANES] = pair
        return carry

    lax.fori_loop(0, units, gather_upstream, 0)

    for t in range(tiles):
        lanes = slice(t * LANES, (t + 1) * LANES)
        mid_a = [tap(0, 0, e, lanes) for e in (-1, 0, 1)]
        off_a = [jnp.where(top, tap(0, 1, e, lanes), tap(0, -1, e, lanes)) for e in (-1, 0, 1)]
        mid_b = [tap(1, 0, 0, lanes), both(1, 0, lanes)]
        off_b = [
            ends(tap(1, 1, 0, lanes), tap(1, -1, 0, lanes)),
            ends(both(1, 1, lanes), both(1, -1, lanes)),
        ]

        def forward(u, carry):
            xs = [cls_ref[slot, :, lanes].astype(jnp.float32) for slot in slots(u)]
            turned = [half_turn(x) for x in xs]
            swapped = [ends_swapped(x, top) for x in xs]
            made_a = [
                sum(
                    mid_a[n] * xs[(k + 2 * n - 2) % 6] + off_a[n] * turned[(k + 2 * n - 2) % 6] for n in range(3)
                )
                for k in range(6)
            ]
            made_b = [
                mid_b[0] * xs[k]
                + mid_b[1] * xs[(k + 3) % 6]
                + off_b[0] * swapped[k]
                + off_b[1] * swapped[(k + 3) % 6]
                for k in range(6)
            ]
            write_pairs(depth, 0, u, lanes, made_a)
            write_pairs(depth, 1, u, lanes, made_b)
            return carry

        lax.fori_loop(0, units, forward, 0, unroll=True)

    for branch in range(2):
        act = jnp.dot(depth[branch], pw_ref[branch], preferred_element_type=jnp.float32)
        act = act + pb_ref[branch : branch + 1, :]
        up = upstream[:, branch * outputs : (branch + 1) * outputs]
        pgrad = (up * gate_slope(act)).astype(jnp.bfloat16)
        point = lax.dot_general(
            depth[branch], pgrad, (((0,), (0,)), ((), ())), preferred_element_type=jnp.float32
        )
        for p in range(16):
            terms[branch, p * shard : p * shard + main, :] = point[p * main : (p + 1) * main]
            terms[branch, p * shard + main : (p + 1) * shard, :] = jnp.zeros((extra, outputs), jnp.float32)
        row = shard_row(9 * per_tap, main, extra)
        terms[branch, row : row + 1, :] = jnp.sum(pgrad.astype(jnp.float32), axis=0, keepdims=True)
        for c in range(0, channels, 384):
            part = lax.dot_general(
                pgrad, pw_ref[branch, c : c + 384, :], (((1,), (1,)), ((), ())), preferred_element_type=jnp.float32
            )
            dgr[branch, :, c : c + 384] = part.astype(jnp.bfloat16)

    for t in range(tiles):
        lanes = slice(t * LANES, (t + 1) * LANES)
        mid_a = [tap(0, 0, e, lanes) for e in (-1, 0, 1)]
        off_a = [jnp.where(top, tap(0, -1, e, lanes), tap(0, 1, e, lanes)) for e in (-1, 0, 1)]
        mid_b = [tap(1, 0, 0, lanes), both(1, 0, lanes)]
        off_b = [
            ends(tap(1, -1, 0, lanes), tap(1, 1, 0, lanes)),
            ends(both(1, -1, lanes), both(1, 1, lanes)),
        ]

        def backward(u, sums):
            sums = list(sums)
            at = slots(u)
            xs = [cls_ref[slot, :, lanes].astype(jnp.float32) for slot in at]
            das = read_pairs(dgr, 0, u, lanes)
            dbs = read_pairs(dgr, 1, u, lanes)
            turned = [half_turn(d) for d in das]
            swapped = [ends_swapped(d, top) for d in dbs]
            for k in range(6):
                made = (
                    sum(
                        mid_a[n] * das[(k - 2 * n + 2) % 6] + off_a[n] * turned[(k - 2 * n + 2) % 6]
                        for n in range(3)
                    )
                    + mid_b[0] * dbs[k]
                    + mid_b[1] * dbs[(k + 3) % 6]
                    + off_b[0] * swapped[k]
                    + off_b[1] * swapped[(k + 3) % 6]
                )
                fg_ref[at[k], :, lanes] = made.astype(jnp.bfloat16)
            for n in range(3):
                sums[n] += sum(xs[(k + 2 * n - 2) % 6] * das[k] for k in range(6))
                sums[3 + n] += sum(xs[(k + 2 * n - 2) % 6] * turned[k] for k in range(6))
            for n in range(2):
                sums[6 + n] += sum(xs[(k + 3 * n) % 6] * dbs[k] for k in range(6))
                sums[8 + n] += sum(xs[(k + 3 * n) % 6] * swapped[k] for k in range(6))
            return tuple(sums)

        zero = jnp.zeros((HELD, LANES), jnp.float32)
        sums = lax.fori_loop(0, units, backward, (zero,) * 10, unroll=True)

        def keep(branch, a, e, value, mask=None):
            value = value if mask is None else jnp.where(mask, value, 0.0)
            row = shard_row(((a + 1) * 3 + e + 1) * per_tap + t // wide, main, extra)
            at = (t % wide) * LANES
            terms[branch, row : row + 1, at : at + LANES] = jnp.sum(value, axis=0, keepdims=True)

        for n in range(3):
            keep(0, 0, n - 1, sums[n])
            keep(0, 1, n - 1, sums[3 + n], jnp.logical_not(top))
            keep(0, -1, n - 1, sums[3 + n], top)
        for e in (-1, 0, 1):
            keep(1, 0, e, sums[6 + abs(e)])
            keep(1, 1, e, sums[8 + abs(e)], end)
            keep(1, -1, e, sums[8 + abs(e)], first)

    @pl.when(core_ref[0] == 0)
    def _():
        kept_ref[...] = terms[0]
        sent_ref[...] = terms[1].astype(jnp.bfloat16)

    @pl.when(core_ref[0] != 0)
    def _():
        kept_ref[...] = terms[1]
        sent_ref[...] = terms[0].astype(jnp.bfloat16)


def per_device(features, depth_w, point_w, point_bias, cotangent):
    _, columns, rows, channels = features.shape
    branches, _, outputs = point_w.shape
    images = lax.axis_size(DP) * features.shape[0]
    plane = lax.axis_size(PLANE)
    core = lax.axis_index("core")
    who = lax.axis_index(LON).reshape(1)
    home, away = deal_units(columns)
    cells = columns * rows
    packed_rows = 16 * (channels // 16 + 8)
    width = channels + cotangent.shape[3]
    act = jnp.bfloat16

    packed = on_chip(
        pack_body,
        jax.ShapeDtypeStruct((PEERS * SLOTS, HELD, width), act),
        (who,),
        [pltpu.with_memory_space_constraint(x, pltpu.HBM) for x in (home, features[0], cotangent[0])],
        (
            pltpu.SMEM(home.shape, jnp.int32),
            pltpu.VMEM((columns, rows, channels), act),
            pltpu.VMEM((columns, rows, cotangent.shape[3]), act),
            pltpu.SemaphoreType.DMA(()),
            pltpu.SemaphoreType.DMA((2, columns)),
        ),
        name="pack",
        space=pltpu.HBM,
    )
    field = exchange(packed.reshape(PEERS, SLOTS, HELD, width), LON).reshape(packed.shape)
    taps = depth_w.astype(jnp.float32).reshape(branches * 9, channels)
    kept, sent, fgrad = on_chip(
        local_body,
        (
            jax.ShapeDtypeStruct((packed_rows, outputs), jnp.float32),
            jax.ShapeDtypeStruct((packed_rows, outputs), act),
            jax.ShapeDtypeStruct((PEERS * SLOTS, HELD, channels), act),
        ),
        (who, core.reshape(1), away),
        (field, taps, point_w, point_bias),
        (
            pltpu.VMEM((branches, cells, channels), act),
            pltpu.VMEM((branches, cells, channels), act),
            pltpu.VMEM((cells, branches * outputs), jnp.float32),
            pltpu.VMEM((branches, packed_rows, outputs), jnp.float32),
        ),
        name="local_work",
    )

    terms = (kept + swap_cores(sent).astype(jnp.float32)).astype(jnp.bfloat16)
    shard = terms.shape[0] // plane
    terms = exchange(terms.reshape(plane, shard, outputs), PLANE)
    terms = sum_pair(jnp.sum(terms.astype(jnp.float32), axis=0), 1)
    fgrad, terms = lax.optimization_barrier((fgrad, terms))
    fgrad = exchange(fgrad.reshape(PEERS, SLOTS, HELD, channels), LON)
    terms = sum_pair(terms, 2)
    terms = sum_ring(terms.astype(jnp.bfloat16), lax.axis_size("zl"))
    fgrad, terms = lax.optimization_barrier((fgrad, terms))
    total = (terms / images).astype(jnp.bfloat16)
    total = gather_copies(total, PLANE)
    feature_grad = on_chip(
        unpack_body,
        jax.ShapeDtypeStruct((columns, rows, channels), act),
        (who, home),
        (fgrad.reshape(PEERS * SLOTS, HELD, channels),),
        name="unpack",
    )[None]
    feature_grad, total = lax.optimization_barrier((feature_grad, total))
    other = swap_cores(total)
    point_grad, depth_grad, bias_grad = on_chip(
        finish_body,
        (
            jax.ShapeDtypeStruct(point_w.shape, act),
            jax.ShapeDtypeStruct((9, branches, channels), act),
            jax.ShapeDtypeStruct(point_bias.shape, jnp.float32),
        ),
        (core.reshape(1),),
        (total, other),
        name="finish",
    )
    depth_grad = depth_grad.reshape(3, 3, branches, channels).transpose(2, 0, 1, 3)
    return (feature_grad, depth_grad, point_grad, bias_grad)


def solution(mesh):
    fine = Mesh(mesh.devices.reshape(4, 4, 2, 2, 4, 2), DP + LON)
    placed = (P(DP, LON, None, None), P(), P(), P(), P(DP, LON, None, None))
    return jax.shard_map(
        per_device,
        mesh=fine,
        in_specs=placed,
        out_specs=(P(DP, LON, None, None), P(), P(), P()),
        check_vma=False,
    )
```

```python
import jax
import jax.numpy as jnp
import numpy as np
from jax import lax
from jax.experimental import pallas as pl
from jax.experimental.pallas import tpu as pltpu
from jax.sharding import Mesh
from jax.sharding import PartitionSpec as P

CLASS = 12
PAIRS = 6
PEERS = 8
SLOTS = 7
HELD = 8
LANES = 128

DP = ("zh", "zl", "xl", "core")
LON = ("y", "xh")
Z = ("zh", "zl")
PLANE = ("xl", "y", "xh")


def swap_cores(block):
    return lax.ppermute(block, "core", [(0, 1), (1, 0)])


def exchange(blocks, axes):
    return lax.all_to_all(blocks, axes, 0, 0, tiled=True)


def gather_copies(block, axes):
    peers = lax.axis_size(axes)
    return exchange(jnp.broadcast_to(block[None], (peers,) + block.shape), axes)


def sum_ring(own, apart):
    planes = lax.axis_size(Z)

    def fetch(block, ahead):
        return lax.ppermute(block, Z, [((i + ahead) % planes, i) for i in range(planes)])

    after = fetch(own, apart)
    before = fetch(own, -apart)
    far = fetch(after, apart)
    own, after, before, far = [x.astype(jnp.float32) for x in (own, after, before, far)]
    return (own + far) + (before + after)


def sum_pair(own, apart):
    planes = lax.axis_size("zl")
    own = own.astype(jnp.bfloat16)
    other = lax.ppermute(own, "zl", [(i, i ^ apart) for i in range(planes)])
    return own.astype(jnp.float32) + other.astype(jnp.float32)


def deal_units(columns):
    blocks = CLASS // 3
    owned = [[] for _ in range(PEERS)]
    for m in range(blocks):
        units = iter([(c, q) for q in range(PAIRS) for c in range(3 * m, 3 * m + 3)])
        for e in range(PEERS):
            owned[e] += [next(units) for _ in range(2 + (e % blocks == m))]
    home = np.zeros((PEERS, columns * PAIRS), np.int32)
    away = np.zeros((PEERS, columns * PAIRS), np.int32)
    used = np.zeros((PEERS, PEERS), np.int32)
    for e in range(PEERS):
        for u, (c, q) in enumerate(owned[e]):
            for k in range(6):
                d, j = divmod(c + CLASS * k, columns)
                home[d, j * PAIRS + q] = e * SLOTS + used[d, e]
                away[e, u * 6 + k] = d * SLOTS + used[d, e]
                used[d, e] += 1
    assert used.max() == SLOTS and used.min() == SLOTS - 1
    return home.reshape(-1), away.reshape(-1)


def blank_slots(ref, lon):
    for block in (3 - lon % 4, 7 - lon % 4):
        ref[block * SLOTS + SLOTS - 1] = jnp.zeros(ref.shape[1:], ref.dtype)


def pack_body(who_ref, home_hbm, feat_hbm, cot_hbm, out_ref, home_ref, feat_ref, cot_ref, table_sem, sems):
    columns, _, channels = feat_ref.shape
    lon = who_ref[0]
    table = pltpu.make_async_copy(home_hbm, home_ref, table_sem)
    table.start()

    def fetch(j):
        return [
            pltpu.make_async_copy(source.at[j], held.at[j], sems.at[n, j])
            for n, (source, held) in enumerate(((feat_hbm, feat_ref), (cot_hbm, cot_ref)))
        ]

    for j in range(columns):
        for copy in fetch(j):
            copy.start()
    blank_slots(out_ref, lon)
    table.wait()

    def column(j, carry):
        for copy in fetch(j):
            copy.wait()
        for source, start in ((feat_ref, 0), (cot_ref, channels)):
            width = source.shape[2]
            rows = source[j].astype(jnp.float32)
            for q in range(PAIRS):
                slot = home_ref[(lon * columns + j) * PAIRS + q]
                tile = jnp.concatenate([rows[12 * n + 2 * q : 12 * n + 2 * q + 2] for n in range(4)], axis=0)
                out_ref[slot, :, start : start + width] = tile.astype(out_ref.dtype)
        return carry

    lax.fori_loop(0, columns, column, 0)


def unpack_body(who_ref, home_ref, tiles_ref, out_ref):
    columns = out_ref.shape[0]
    lon = who_ref[0]

    def column(j, carry):
        tiles = [tiles_ref[home_ref[(lon * columns + j) * PAIRS + q]].astype(jnp.float32) for q in range(PAIRS)]
        rows = [tiles[q][2 * n : 2 * n + 2] for n in range(4) for q in range(PAIRS)]
        out_ref[j] = jnp.concatenate(rows, axis=0).astype(out_ref.dtype)
        return carry

    lax.fori_loop(0, columns, column, 0)


def finish_body(core_ref, mine_ref, other_ref, point_ref, taps_ref, bias_ref):
    shards, held, outputs = mine_ref.shape
    channels = point_ref.shape[1]
    main = channels // shards
    per_tap = -(-channels // outputs)

    def branch_out(branch, source):
        for p in range(shards):
            point_ref[branch, p * main : (p + 1) * main, :] = source[p, :main]

        def extra(row):
            return source[row // (held - main), main + row % (held - main)].astype(jnp.float32)

        for n in range(9):
            for c in range(per_tap):
                width = min(outputs, channels - c * outputs)
                row = extra(n * per_tap + c)[:width]
                taps_ref[n, branch, c * outputs : c * outputs + width] = row.astype(taps_ref.dtype)
        bias_ref[branch] = extra(9 * per_tap)

    for first in (0, 1):

        @pl.when(core_ref[0] == first)
        def _():
            branch_out(first, mine_ref)
            branch_out(1 - first, other_ref)


def on_chip(body, out_shape, scalars, arrays, scratch=(), name=None, space=pltpu.VMEM):
    vmem = pl.BlockSpec(memory_space=pltpu.VMEM)
    smem = pl.BlockSpec(memory_space=pltpu.SMEM)
    return pl.pallas_call(
        body,
        out_shape=out_shape,
        in_specs=[smem] * len(scalars) + [pl.BlockSpec(memory_space=space)] * len(arrays),
        out_specs=jax.tree.map(lambda _: vmem, out_shape),
        scratch_shapes=list(scratch),
        compiler_params=pltpu.CompilerParams(vmem_limit_bytes=48 << 20),
        name=name,
    )(*scalars, *arrays)


def gate_slope(pre_act):
    sigmoid_val = jax.nn.sigmoid(pre_act)
    return sigmoid_val * (1.0 + pre_act * (1.0 - sigmoid_val))


def half_turn(tile):
    return pltpu.roll(tile, 4, 0)


def ends_swapped(tile, top):
    return jnp.where(top, pltpu.roll(tile, 2, 0), pltpu.roll(tile, 6, 0))


def shard_row(row, main, extra):
    return (row // extra) * (main + extra) + main + row % extra


def local_body(
    who_ref, core_ref, away_ref, cls_ref, taps_ref, pw_ref, pb_ref, kept_ref, sent_ref, fg_ref, depth, dgr, upstream, terms
):
    channels, outputs = pw_ref.shape[1:]
    shard = terms.shape[1] // 16
    main = channels // 16
    extra = shard - main
    tiles = channels // LANES
    wide = outputs // LANES
    per_tap = -(-tiles // wide)
    sub = lax.broadcasted_iota(jnp.int32, (HELD, LANES), 0)
    top = sub < 4
    first = sub < 2
    end = sub >= 6

    def tap(branch, a, e, lanes):
        row = branch * 9 + (a + 1) * 3 + e + 1
        return jnp.broadcast_to(taps_ref[row : row + 1, lanes], (HELD, LANES))

    def ends(up, down):
        return jnp.where(first, up, jnp.where(end, down, 0.0))

    def both(branch, a, lanes):
        return tap(branch, a, -1, lanes) + tap(branch, a, 1, lanes)

    units = depth.shape[1] // (6 * HELD)
    lon = who_ref[0]
    blank_slots(fg_ref, lon)

    def slots(u):
        return [away_ref[(lon * units + u) * 6 + k] for k in range(6)]

    def pair_rows(u, k):
        return pl.ds(pl.multiple_of((u * 6 + k) * HELD, 16), 16)

    def read_pairs(ref, branch, u, lanes):
        out = []
        for k in range(0, 6, 2):
            pair = ref[branch, pair_rows(u, k), lanes].astype(jnp.float32)
            out += [pair[:HELD], pair[HELD:]]
        return out

    def write_pairs(ref, branch, u, lanes, made):
        for k in range(0, 6, 2):
            pair = jnp.concatenate([made[k], made[k + 1]], axis=0)
            ref[branch, pair_rows(u, k), lanes] = pair.astype(jnp.bfloat16)

    def gather_upstream(u, carry):
        at = slots(u)
        for k in range(0, 6, 2):
            for c in range(channels, cls_ref.shape[2], LANES):
                lanes = slice(c, c + LANES)
                pair = jnp.concatenate([cls_ref[at[k + n], :, lanes].astype(jnp.float32) for n in range(2)], axis=0)
                upstream[pair_rows(u, k), c - channels : c - channels + LANES] = pair
        return carry

    lax.fori_loop(0, units, gather_upstream, 0)

    for t in range(tiles):
        lanes = slice(t * LANES, (t + 1) * LANES)
        mid_a = [tap(0, 0, e, lanes) for e in (-1, 0, 1)]
        off_a = [jnp.where(top, tap(0, 1, e, lanes), tap(0, -1, e, lanes)) for e in (-1, 0, 1)]
        mid_b = [tap(1, 0, 0, lanes), both(1, 0, lanes)]
        off_b = [
            ends(tap(1, 1, 0, lanes), tap(1, -1, 0, lanes)),
            ends(both(1, 1, lanes), both(1, -1, lanes)),
        ]

        def forward(u, carry):
            xs = [cls_ref[slot, :, lanes].astype(jnp.float32) for slot in slots(u)]
            turned = [half_turn(x) for x in xs]
            swapped = [ends_swapped(x, top) for x in xs]
            made_a = [
                sum(
                    mid_a[n] * xs[(k + 2 * n - 2) % 6] + off_a[n] * turned[(k + 2 * n - 2) % 6] for n in range(3)
                )
                for k in range(6)
            ]
            made_b = [
                mid_b[0] * xs[k]
                + mid_b[1] * xs[(k + 3) % 6]
                + off_b[0] * swapped[k]
                + off_b[1] * swapped[(k + 3) % 6]
                for k in range(6)
            ]
            write_pairs(depth, 0, u, lanes, made_a)
            write_pairs(depth, 1, u, lanes, made_b)
            return carry

        lax.fori_loop(0, units, forward, 0, unroll=True)

    for branch in range(2):
        act = jnp.dot(depth[branch], pw_ref[branch], preferred_element_type=jnp.float32)
        act = act + pb_ref[branch : branch + 1, :]
        up = upstream[:, branch * outputs : (branch + 1) * outputs]
        pgrad = (up * gate_slope(act)).astype(jnp.bfloat16)
        point = lax.dot_general(
            depth[branch], pgrad, (((0,), (0,)), ((), ())), preferred_element_type=jnp.float32
        )
        for p in range(16):
            terms[branch, p * shard : p * shard + main, :] = point[p * main : (p + 1) * main]
            terms[branch, p * shard + main : (p + 1) * shard, :] = jnp.zeros((extra, outputs), jnp.float32)
        row = shard_row(9 * per_tap, main, extra)
        terms[branch, row : row + 1, :] = jnp.sum(pgrad.astype(jnp.float32), axis=0, keepdims=True)
        for c in range(0, channels, 384):
            part = lax.dot_general(
                pgrad, pw_ref[branch, c : c + 384, :], (((1,), (1,)), ((), ())), preferred_element_type=jnp.float32
            )
            dgr[branch, :, c : c + 384] = part.astype(jnp.bfloat16)

    for t in range(tiles):
        lanes = slice(t * LANES, (t + 1) * LANES)
        mid_a = [tap(0, 0, e, lanes) for e in (-1, 0, 1)]
        off_a = [jnp.where(top, tap(0, -1, e, lanes), tap(0, 1, e, lanes)) for e in (-1, 0, 1)]
        mid_b = [tap(1, 0, 0, lanes), both(1, 0, lanes)]
        off_b = [
            ends(tap(1, -1, 0, lanes), tap(1, 1, 0, lanes)),
            ends(both(1, -1, lanes), both(1, 1, lanes)),
        ]

        def backward(u, sums):
            sums = list(sums)
            at = slots(u)
            xs = [cls_ref[slot, :, lanes].astype(jnp.float32) for slot in at]
            das = read_pairs(dgr, 0, u, lanes)
            dbs = read_pairs(dgr, 1, u, lanes)
            turned = [half_turn(d) for d in das]
            swapped = [ends_swapped(d, top) for d in dbs]
            for k in range(6):
                made = (
                    sum(
                        mid_a[n] * das[(k - 2 * n + 2) % 6] + off_a[n] * turned[(k - 2 * n + 2) % 6]
                        for n in range(3)
                    )
                    + mid_b[0] * dbs[k]
                    + mid_b[1] * dbs[(k + 3) % 6]
                    + off_b[0] * swapped[k]
                    + off_b[1] * swapped[(k + 3) % 6]
                )
                fg_ref[at[k], :, lanes] = made.astype(jnp.bfloat16)
            for n in range(3):
                sums[n] += sum(xs[(k + 2 * n - 2) % 6] * das[k] for k in range(6))
                sums[3 + n] += sum(xs[(k + 2 * n - 2) % 6] * turned[k] for k in range(6))
            for n in range(2):
                sums[6 + n] += sum(xs[(k + 3 * n) % 6] * dbs[k] for k in range(6))
                sums[8 + n] += sum(xs[(k + 3 * n) % 6] * swapped[k] for k in range(6))
            return tuple(sums)

        zero = jnp.zeros((HELD, LANES), jnp.float32)
        sums = lax.fori_loop(0, units, backward, (zero,) * 10, unroll=True)

        def keep(branch, a, e, value, mask=None):
            value = value if mask is None else jnp.where(mask, value, 0.0)
            row = shard_row(((a + 1) * 3 + e + 1) * per_tap + t // wide, main, extra)
            at = (t % wide) * LANES
            terms[branch, row : row + 1, at : at + LANES] = jnp.sum(value, axis=0, keepdims=True)

        for n in range(3):
            keep(0, 0, n - 1, sums[n])
            keep(0, 1, n - 1, sums[3 + n], jnp.logical_not(top))
            keep(0, -1, n - 1, sums[3 + n], top)
        for e in (-1, 0, 1):
            keep(1, 0, e, sums[6 + abs(e)])
            keep(1, 1, e, sums[8 + abs(e)], end)
            keep(1, -1, e, sums[8 + abs(e)], first)

    @pl.when(core_ref[0] == 0)
    def _():
        kept_ref[...] = terms[0]
        sent_ref[...] = terms[1].astype(jnp.bfloat16)

    @pl.when(core_ref[0] != 0)
    def _():
        kept_ref[...] = terms[1]
        sent_ref[...] = terms[0].astype(jnp.bfloat16)


def per_device(features, depth_w, point_w, point_bias, cotangent):
    _, columns, rows, channels = features.shape
    branches, _, outputs = point_w.shape
    images = lax.axis_size(DP) * features.shape[0]
    plane = lax.axis_size(PLANE)
    core = lax.axis_index("core")
    who = lax.axis_index(LON).reshape(1)
    home, away = deal_units(columns)
    cells = columns * rows
    packed_rows = 16 * (channels // 16 + 8)
    width = channels + cotangent.shape[3]
    act = jnp.bfloat16

    packed = on_chip(
        pack_body,
        jax.ShapeDtypeStruct((PEERS * SLOTS, HELD, width), act),
        (who,),
        [pltpu.with_memory_space_constraint(x, pltpu.HBM) for x in (home, features[0], cotangent[0])],
        (
            pltpu.SMEM(home.shape, jnp.int32),
            pltpu.VMEM((columns, rows, channels), act),
            pltpu.VMEM((columns, rows, cotangent.shape[3]), act),
            pltpu.SemaphoreType.DMA(()),
            pltpu.SemaphoreType.DMA((2, columns)),
        ),
        name="pack",
        space=pltpu.HBM,
    )
    field = exchange(packed.reshape(PEERS, SLOTS, HELD, width), LON).reshape(packed.shape)
    taps = depth_w.astype(jnp.float32).reshape(branches * 9, channels)
    kept, sent, fgrad = on_chip(
        local_body,
        (
            jax.ShapeDtypeStruct((packed_rows, outputs), jnp.float32),
            jax.ShapeDtypeStruct((packed_rows, outputs), act),
            jax.ShapeDtypeStruct((PEERS * SLOTS, HELD, channels), act),
        ),
        (who, core.reshape(1), away),
        (field, taps, point_w, point_bias),
        (
            pltpu.VMEM((branches, cells, channels), act),
            pltpu.VMEM((branches, cells, channels), act),
            pltpu.VMEM((cells, branches * outputs), jnp.float32),
            pltpu.VMEM((branches, packed_rows, outputs), jnp.float32),
        ),
        name="local_work",
    )

    terms = (kept + swap_cores(sent).astype(jnp.float32)).astype(jnp.bfloat16)
    shard = terms.shape[0] // plane
    terms = exchange(terms.reshape(plane, shard, outputs), PLANE)
    fgrad, terms = lax.optimization_barrier((fgrad, terms))
    fgrad = exchange(fgrad.reshape(PEERS, SLOTS, HELD, channels), LON)
    terms = jnp.sum(terms.astype(jnp.float32), axis=0)
    terms = sum_ring(terms.astype(jnp.bfloat16), lax.axis_size("zl"))
    terms = sum_pair(sum_pair(terms, 2), 1)
    fgrad, terms = lax.optimization_barrier((fgrad, terms))
    total = (terms / images).astype(jnp.bfloat16)
    total = gather_copies(total, PLANE)
    feature_grad = on_chip(
        unpack_body,
        jax.ShapeDtypeStruct((columns, rows, channels), act),
        (who, home),
        (fgrad.reshape(PEERS * SLOTS, HELD, channels),),
        name="unpack",
    )[None]
    feature_grad, total = lax.optimization_barrier((feature_grad, total))
    other = swap_cores(total)
    point_grad, depth_grad, bias_grad = on_chip(
        finish_body,
        (
            jax.ShapeDtypeStruct(point_w.shape, act),
            jax.ShapeDtypeStruct((9, branches, channels), act),
            jax.ShapeDtypeStruct(point_bias.shape, jnp.float32),
        ),
        (core.reshape(1),),
        (total, other),
        name="finish",
    )
    depth_grad = depth_grad.reshape(3, 3, branches, channels).transpose(2, 0, 1, 3)
    return (feature_grad, depth_grad, point_grad, bias_grad)


def solution(mesh):
    fine = Mesh(mesh.devices.reshape(4, 4, 2, 2, 4, 2), DP + LON)
    placed = (P(DP, LON, None, None), P(), P(), P(), P(DP, LON, None, None))
    return jax.shard_map(
        per_device,
        mesh=fine,
        in_specs=placed,
        out_specs=(P(DP, LON, None, None), P(), P(), P()),
        check_vma=False,
    )
```
